512 devices in a mesh: sub: 64 (over z, y), harm: 8 (over x, core).
Axes of the slice: x: 4, y: 4, z: 16, core: 2. Of those that a mesh axis runs over, the one named last changes fastest.
Arguments:
- flex: float32 [64, 8, 768, 768], P('sub', 'harm'), may hold values from -1 to 4, as said below
- loads: float32 [64, 8, 768, 256], P('sub', 'harm'), may hold values from -4 to 4
- side: int32 [64, 12], P('sub'), may hold values from -1 to 1, as said below
- partner: int32 [64, 12], P('sub'), may hold values from 0 to 11, as said below
- contact_blocks: int32 [64, 4], P('sub'), may hold values from 0 to 11, all different within a row
- contact_stiff: float32 [64, 256], P('sub'), may hold values from 0.01 to 0.1
Outputs:
- multipliers: float32 [64, 8, 768, 256], P('sub', 'harm')
- contact_force: float32 [64, 8, 256, 256], P('sub', 'harm')
The draws below stay inside these ranges and needn't reach their ends.
Inputs may be any that keep to these rules, and one draw needn't show every extreme that they name: Block b of subdomain s is shared with subdomain s + 1 (cyclic) where side is 1, with s - 1 where it is -1, with none where it is 0. Each subdomain shares 1 to 4 blocks with each neighbour, and the pairing through partner is mutual. `partner`: A block with side 0 names itself. `flex`: symmetric positive definite.
All inputs are finite; a program needn't handle non-finite values.
Results may differ from the reference program's by a relative error of at most 0.0003.
Values sent between devices are 32-bit elements; how exact they have to be, the bound alone decides.
A program may use at most 64 MiB of HBM per device.

```python
import math
import jax
import jax.numpy as jnp
from jax import lax

IFACE = 768
HARMS = 8
TIMES = 64
CASES = 128
BLK = 64
MAXB = 4
CB = 4
ROUNDS = 2
UPDATES = 2
SUBS = 64
NBLK = 12
CROWS = 256


def draw_flex(key, part):
    key_gram, key_diag, key_couple = jax.random.split(jax.random.fold_in(key, 3), 3)
    factors = jax.random.normal(key_gram, (SUBS, IFACE, IFACE), jnp.float32)
    diag_part = jax.random.uniform(key_diag, (SUBS, HARMS, IFACE), jnp.float32, 0.5, 1.5)
    gram_part = lax.map(lambda one: jnp.dot(one, one.T, precision=lax.Precision.HIGHEST) / IFACE, factors)
    coupling = jnp.exp(jax.random.uniform(key_couple, (SUBS, HARMS), jnp.float32, math.log(0.3), 0.0))
    identity_mat = jnp.eye(IFACE, dtype=jnp.float32)
    return diag_part[..., None] * identity_mat + coupling[..., None, None] * gram_part[:, None]


def draw_loads(key, part):
    key_values = jax.random.fold_in(jax.random.fold_in(key, 11), 0)
    shape = (SUBS, HARMS, IFACE, 2 * CASES)
    sub_level = 0.25 + 0.5 * jnp.arange(SUBS, dtype=jnp.float32) / (SUBS - 1)
    values = jnp.clip(jax.random.normal(key_values, shape, jnp.float32), -5.0, 5.0)
    return values * sub_level[:, None, None, None]


def pairing(key):
    key_counts, key_perm, key_spot = jax.random.split(jax.random.fold_in(key, 7), 3)
    block_count = IFACE // BLK
    shared = jax.random.randint(key_counts, (SUBS,), 1, MAXB + 1).astype(jnp.int32)
    full_spot = jax.random.randint(key_spot, (), 0, SUBS)
    subs_index = jnp.arange(SUBS, dtype=jnp.int32)
    shared = jnp.where(subs_index == full_spot, MAXB, shared).astype(jnp.int32)
    perm_keys = jax.random.split(key_perm, SUBS)
    layout = jax.vmap(lambda one: jax.random.permutation(one, block_count))(perm_keys).astype(jnp.int32)
    after = (subs_index + 1) % SUBS
    before = (subs_index - 1) % SUBS
    place = jnp.arange(block_count, dtype=jnp.int32)[None, :]
    right_mark = place < shared[:, None]
    left_mark = (place >= shared[:, None]) & (place < shared[:, None] + shared[before][:, None])
    right_index = jnp.clip(shared[after][:, None] + place, 0, block_count - 1)
    right_partner = jnp.take_along_axis(layout[after], right_index, axis=1)
    left_index = jnp.clip(place - shared[:, None], 0, block_count - 1)
    left_partner = jnp.take_along_axis(layout[before], left_index, axis=1)
    side_place = jnp.where(right_mark, 1, jnp.where(left_mark, -1, 0)).astype(jnp.int32)
    partner_place = jnp.where(right_mark, right_partner, jnp.where(left_mark, left_partner, layout)).astype(jnp.int32)
    row_index = jnp.broadcast_to(subs_index[:, None], layout.shape)
    side = jnp.zeros((SUBS, block_count), jnp.int32).at[row_index, layout].set(side_place)
    partner = jnp.zeros((SUBS, block_count), jnp.int32).at[row_index, layout].set(partner_place)
    return (side, partner)


def draw_side(key, part):
    return pairing(key)[0]


def draw_partner(key, part):
    return pairing(key)[1]


def block_levels(key, extent, cuts, least, high):
    def one(dim, parts):
        heights = jax.random.uniform(jax.random.fold_in(jax.random.fold_in(key, 6), dim), (parts,), jnp.float32, least / len(cuts), high / len(cuts))
        return jnp.repeat(jnp.exp(heights), extent[dim] // parts).reshape((-1,) + (1,) * (len(extent) - dim - 1))

    gain = one(*cuts[0])
    for cut in cuts[1:]:
        gain = gain * one(*cut)
    return gain


def picks_of(rng, rows, count, top, lift):
    order = jax.random.permutation(jax.random.fold_in(rng, 1), count)
    boost = order
    for power in range(3):
        boost = boost * boost // count
    boost = boost * lift // count
    tickets = jax.random.randint(jax.random.fold_in(rng, 2), (rows, count), 0, 4096) + boost
    holders = jax.random.permutation(jax.random.fold_in(rng, 3), rows)[jnp.arange(count) % rows]
    tickets = jnp.where(jnp.arange(rows)[:, None] == holders[None, :], 1 << 14, tickets)
    priority = tickets * count + jnp.arange(count)
    return lax.top_k(priority.astype(jnp.int32), top)[1].astype(jnp.int32)


def setup_inputs(seed: int = 0) -> dict:
    key_of = jax.random.split(jax.random.key(seed), 7)
    flex = draw_flex(jax.random.fold_in(key_of[6], 71), 0)
    loads = draw_loads(jax.random.fold_in(key_of[6], 71), 0)
    side = draw_side(jax.random.fold_in(key_of[6], 71), 0)
    partner = draw_partner(jax.random.fold_in(key_of[6], 71), 0)
    contact_blocks = picks_of(key_of[4], SUBS, NBLK, CB, 0)
    contact_stiff = jnp.clip(jnp.exp(math.log(0.1) - 2.3025851 * jax.random.uniform(key_of[5], (SUBS, CROWS), jnp.float32) ** block_levels(key_of[5], (SUBS, CROWS), ((0, 64),), -0.2, 0.2)), 0.01, 0.1)
    return {"flex": flex, "loads": loads, "side": side, "partner": partner, "contact_blocks": contact_blocks, "contact_stiff": contact_stiff}


precise = lax.Precision.HIGHEST
tiny_value = 1e-6


def wave_tables():
    time_points = jnp.arange(TIMES, dtype=jnp.float32)
    harm_orders = jnp.arange(1, HARMS + 1, dtype=jnp.float32)
    phases = (2.0 * math.pi / TIMES) * time_points[:, None] * harm_orders[None, :]
    return jnp.cos(phases), jnp.sin(phases)


def apply_flex(flex, field):
    return jnp.einsum("shij,shjc->shic", flex, field, precision=precise)


def opposite(trace, side, partner):
    sub_count = trace.shape[0]
    blocks = trace.reshape(sub_count, HARMS, IFACE // BLK, BLK, 2 * CASES)
    source_sub = (jnp.arange(sub_count, dtype=jnp.int32)[:, None] + side) % sub_count
    picked = blocks[source_sub, :, partner]
    return jnp.transpose(picked, (0, 2, 1, 3, 4)).reshape(trace.shape)


def cubic_cycle(contact_coef, contact_stiff):
    cos_table, sin_table = wave_tables()
    sub_count = contact_coef.shape[0]
    shaped = contact_coef.reshape(sub_count, HARMS, CB * BLK, CASES, 2)
    signal = jnp.einsum("tk,skrn->strn", cos_table, shaped[..., 0], precision=precise)
    signal = signal + jnp.einsum("tk,skrn->strn", sin_table, shaped[..., 1], precision=precise)
    cubic_term = signal * signal * signal
    cos_coef = (2.0 / TIMES) * jnp.einsum("tk,strn->skrn", cos_table, cubic_term, precision=precise)
    sin_coef = (2.0 / TIMES) * jnp.einsum("tk,strn->skrn", sin_table, cubic_term, precision=precise)
    force = jnp.stack([cos_coef, sin_coef], axis=-1).reshape(contact_coef.shape)
    return force * contact_stiff[:, None, :, None]


def reference(flex, loads, side, partner, contact_blocks, contact_stiff):
    sub_count = loads.shape[0]
    sub_rows = jnp.arange(sub_count, dtype=jnp.int32)[:, None]
    block_shape = (sub_count, HARMS, IFACE // BLK, BLK, 2 * CASES)
    multipliers = jnp.zeros_like(loads)
    trace = loads
    contact_force = None
    for outer in range(ROUNDS):
        if outer > 0:
            trace = apply_flex(flex, multipliers) + loads
        for inner in range(UPDATES):
            jump = trace - opposite(trace, side, partner)
            flex_image = apply_flex(flex, jump)
            squares = jnp.sum(jump * jump, axis=(0, 2))
            curvature = jnp.sum(jump * flex_image, axis=(0, 2))
            step_size = (squares / (curvature + tiny_value))[None, :, None, :]
            multipliers = multipliers - step_size * jump
            trace = trace - step_size * flex_image
        picked = trace.reshape(block_shape)[sub_rows, :, contact_blocks]
        contact_coef = jnp.transpose(picked, (0, 2, 1, 3, 4)).reshape(sub_count, HARMS, CB * BLK, 2 * CASES)
        contact_force = cubic_cycle(contact_coef, contact_stiff)
        returned = jnp.transpose(contact_force.reshape(sub_count, HARMS, CB, BLK, 2 * CASES), (0, 2, 1, 3, 4))
        multipliers = multipliers.reshape(block_shape).at[sub_rows, :, contact_blocks].add(-returned).reshape(loads.shape)
    return multipliers, contact_force
```

```python
import functools
import math

import jax
import jax.numpy as jnp
from jax import lax
from jax.experimental import pallas as pl
from jax.experimental.pallas import tpu as pltpu
from jax.sharding import PartitionSpec as P

MESH = pl.DeviceIdType.MESH
TIMES = 64
ROUNDS = 2
TINY = 1e-6
NB = 12
BLK = 64
ROWS = NB * BLK
COLS = 256
MAXB = 4
CB = 4
CROWS = CB * BLK
NY = 4
CHUNKS = 2
TILE = 384

f32 = jnp.float32
bf16 = jnp.bfloat16


def dot(a, b):
    return jnp.dot(a, b, preferred_element_type=f32)


def split(x):
    high = x.astype(bf16)
    return high, (x - high.astype(f32)).astype(bf16)


def split3(x):
    high = x.astype(bf16)
    rest = x - high.astype(f32)
    middle = rest.astype(bf16)
    return high, middle, (rest - middle.astype(f32)).astype(bf16)


def contact_law(cos_coef, sin_coef, harms):
    half = TIMES // 2
    cos_out = [None] * harms
    sin_out = [None] * harms

    def add(out, k, value, factor):
        if abs(factor) > 1e-9:
            term = value * factor
            out[k] = term if out[k] is None else out[k] + term

    def total(coefs, table, parity):
        result = None
        for k in range(harms):
            if (k + 1) % 2 == parity and abs(table[k]) > 1e-9:
                term = coefs[k] * table[k]
                result = term if result is None else result + term
        return jnp.zeros_like(coefs[0]) if result is None else result

    def cubes(even, odd):
        even2, odd2 = even * even, odd * odd
        return even * (even2 + 3.0 * odd2), odd * (odd2 + 3.0 * even2)

    for t in range(TIMES // 4 + 1):
        cos_t = [math.cos(2 * math.pi * t * (k + 1) / TIMES) for k in range(harms)]
        sin_t = [math.sin(2 * math.pi * t * (k + 1) / TIMES) for k in range(harms)]
        pe, po = total(cos_coef, cos_t, 0), total(cos_coef, cos_t, 1)
        qe, qo = total(sin_coef, sin_t, 0), total(sin_coef, sin_t, 1)
        u1, d1 = cubes(pe + po, qe + qo)
        scale = 2.0 * 2.0 / TIMES
        if t == 0:
            scale *= 0.5
        if t == TIMES // 4:
            scale *= 0.5
        u2, d2 = cubes(pe - po, qo - qe)
        up, um, dp, dm = u1 + u2, u1 - u2, d1 + d2, d1 - d2
        for k in range(harms):
            even = (k + 1) % 2 == 0
            add(cos_out, k, up if even else um, scale * cos_t[k])
            add(sin_out, k, dm if even else dp, scale * sin_t[k])
    return cos_out, sin_out


def kernel(nz, harms, side, partner, cblk, stiff, flex, loads, mult, force, *scratch):
    names = iter(scratch)
    nch = CHUNKS
    width = COLS // nch
    part = CROWS // harms
    flex_v, fh, fl, ld, tr, im, gg, jj, dv, mm, xh, xl, cf, stc, perm, perm_t, tab = (
        next(names) for _ in range(17)
    )
    grid = lambda n: [[next(names) for _ in range(nch)] for _ in range(n)]
    snd, rcv = grid(2 * ROUNDS), grid(2 * ROUNDS)
    sum_y, sum_z = grid(ROUNDS), grid(ROUNDS)
    ct, rc, oc, bc = grid(ROUNDS), grid(ROUNDS), grid(ROUNDS), grid(ROUNDS)
    in_sem, out_sem, ex_s, ex_r, y_s, y_r, z_s, z_r, a_s, a_r = names

    sub = lax.axis_index("sub")
    harm = lax.axis_index("harm")
    subs = nz * NY
    my_y = lax.rem(sub, NY)
    my_z = sub // NY
    right = (lax.rem(sub + 1, subs), harm)
    left = (lax.rem(sub + subs - 1, subs), harm)
    y_peers = [my_z * NY + lax.rem(my_y + d, NY) for d in range(1, NY)]
    z_order = sorted(range(1, nz), key=lambda d: -min(d, nz - d))
    z_peers = {d: lax.rem(my_z + d, nz) * NY + my_y for d in z_order}
    h_order = sorted(range(1, harms), key=lambda d: -min(d, harms - d))
    h_peers = {d: lax.rem(harm + d, harms) for d in h_order}

    barrier = pltpu.get_barrier_semaphore()
    greet = [right, left]
    greet += [(p, harm) for p in y_peers] + [(z_peers[d], harm) for d in z_order]
    greet += [(sub, h_peers[d]) for d in h_order]
    for peer in greet:
        pl.semaphore_signal(barrier, inc=1, device_id=peer, device_id_type=MESH)

    in_copies = [
        pltpu.make_async_copy(loads.at[:, :, pl.ds(c * width, width)], ld.at[c], in_sem.at[c])
        for c in range(nch)
    ]
    in_copies.append(pltpu.make_async_copy(flex, flex_v, in_sem.at[nch]))
    for copy in in_copies:
        copy.start()

    sides = [side[0, b] for b in range(NB)]
    partners = [partner[0, b] for b in range(NB)]
    contacts = [cblk[0, q] for q in range(CB)]
    for way, sign in enumerate((1, -1)):
        count = jnp.int32(0)
        picks = [jnp.int32(0)] * MAXB
        for b in range(NB):
            hit = sides[b] == sign
            picks = [jnp.where(hit & (count == k), b, picks[k]) for k in range(MAXB)]
            count = count + jnp.where(hit, 1, 0)
        for k in range(MAXB):
            tab[4, way * MAXB + k] = picks[k]
    for b in range(NB):
        slot = jnp.int32(0)
        for other in range(NB):
            if other != b:
                before = (sides[other] == sides[b]) & (partners[other] < partners[b])
                slot = slot + jnp.where(before, 1, 0)
        slot = jnp.minimum(slot, MAXB - 1)
        slot = jnp.where(sides[b] == 1, slot + MAXB, slot)
        tab[0, b] = slot
        tab[1, b] = jnp.where(sides[b] != 0, 1, 0)
        place = jnp.int32(0)
        found = jnp.int32(0)
        for q in range(CB):
            same = contacts[q] == b
            place = jnp.where(same, q, place)
            found = jnp.where(same, 1, found)
        tab[2, b] = place
        tab[3, b] = found

    row = lax.broadcasted_iota(jnp.int32, (COLS, COLS), 0)
    col = lax.broadcasted_iota(jnp.int32, (COLS, COLS), 1)
    place = lambda a: 128 * (a % 2) + 64 * (a // 128) + (a % 128) // 2
    perm[...] = jnp.where(place(row) == col, 1.0, 0.0).astype(bf16)
    perm_t[...] = jnp.where(place(col) == row, 1.0, 0.0).astype(bf16)
    column = jnp.sum(jnp.where(row == col, stiff[...], 0.0), axis=1, keepdims=True)
    stc[...] = jnp.broadcast_to(column, (CROWS, width))

    for copy in in_copies:
        copy.wait()

    @pl.loop(0, NB)
    def _(b):
        rows = pl.ds(pl.multiple_of(b * BLK, BLK), BLK)
        fh[rows, :], fl[rows, :] = split(flex_v[rows, :])

    pl.semaphore_wait(barrier, len(greet))

    def exchange(e, c, way):
        peer = right if way == 0 else left
        return pltpu.make_async_remote_copy(
            src_ref=snd[e][c].at[pl.ds(way * MAXB, MAXB)],
            dst_ref=rcv[e][c].at[pl.ds(way * MAXB, MAXB)],
            send_sem=ex_s.at[e, c, way],
            recv_sem=ex_r.at[e, c, way],
            device_id=peer,
            device_id_type=MESH,
        )

    def send_blocks(e, c, source):
        for way in range(2):
            for k in range(way * MAXB, (way + 1) * MAXB):
                snd[e][c][k] = source[c, tab[4, k]]
            exchange(e, c, way).start()

    def fold(x):
        return jnp.sum(x.reshape(BLK // 8, 8, width), axis=0)

    def difference(e, c, source, target):
        for way in range(2):
            exchange(e, c, way).wait_recv()

        def step(b, acc):
            value = source[c, b] - rcv[e][c][tab[0, b]]
            value = jnp.where(tab[1, b] != 0, value, 0.0)
            target[c, b] = value
            xh[c, b], xl[c, b] = split(value)
            return acc + fold(value * value)

        acc = lax.fori_loop(0, NB, step, jnp.zeros((8, width), f32))
        return jnp.sum(acc, axis=0, keepdims=True)

    def product(c, target, subtract=False):
        high = xh[c].reshape(ROWS, width)
        low = xl[c].reshape(ROWS, width)
        count = TILE // BLK

        @pl.loop(0, ROWS // TILE)
        def _(i):
            rows = pl.ds(pl.multiple_of(i * TILE, TILE), TILE)
            blocks = pl.ds(i * count, count)
            first = fh[rows, :]
            out = dot(first, high) + (dot(first, low) + dot(fl[rows, :], high))
            out = out.reshape(count, BLK, width)
            target[c, blocks] = target[c, blocks] - out if subtract else out

    def inner(c, one, two):
        def step(b, acc):
            return acc + fold(one[c, b] * two[c, b])

        acc = lax.fori_loop(0, NB, step, jnp.zeros((8, width), f32))
        return jnp.sum(acc, axis=0, keepdims=True)

    def y_copy(r, c, d):
        ref = sum_y[r][c].at[my_y]
        return pltpu.make_async_remote_copy(
            src_ref=ref,
            dst_ref=ref,
            send_sem=y_s.at[r, c, d],
            recv_sem=y_r.at[r, c, d],
            device_id=(y_peers[d - 1], harm),
            device_id_type=MESH,
        )

    def z_copy(r, c, d):
        ref = sum_z[r][c].at[my_z]
        return pltpu.make_async_remote_copy(
            src_ref=ref,
            dst_ref=ref,
            send_sem=z_s.at[r, c, d],
            recv_sem=z_r.at[r, c, d],
            device_id=(z_peers[d], harm),
            device_id_type=MESH,
        )

    def rows_of(index):
        return pl.ds(pl.multiple_of(index * part, part), part)

    def to_harm(r, c, d):
        return pltpu.make_async_remote_copy(
            src_ref=ct[r][c].at[rows_of(h_peers[d])],
            dst_ref=rc[r][c].at[harm],
            send_sem=a_s.at[r, c, 0, d],
            recv_sem=a_r.at[r, c, 0, d],
            device_id=(sub, h_peers[d]),
            device_id_type=MESH,
        )

    def from_harm(r, c, d):
        return pltpu.make_async_remote_copy(
            src_ref=oc[r][c].at[h_peers[d]],
            dst_ref=bc[r][c].at[rows_of(harm)],
            send_sem=a_s.at[r, c, 1, d],
            recv_sem=a_r.at[r, c, 1, d],
            device_id=(sub, h_peers[d]),
            device_id_type=MESH,
        )

    def contact(r, c):
        strips = part // (8 * nch)

        def piece(k, i):
            both = [
                rc[r][c][k, pl.ds(pl.multiple_of((i + n * strips) * 8, 8), 8), :]
                for n in range(nch)
            ]
            return jnp.concatenate(both, axis=1) if nch > 1 else both[0]

        @pl.loop(0, strips)
        def _(i):
            rows = jnp.concatenate([piece(k, i) for k in range(harms)], axis=0)
            high, middle, low = split3(rows)
            p = perm[...]
            flat = dot(high, p) + (dot(middle, p) + dot(low, p))
            cos_coef = [flat[8 * k : 8 * k + 8, :128] for k in range(harms)]
            sin_coef = [flat[8 * k : 8 * k + 8, 128:] for k in range(harms)]
            cos_out, sin_out = contact_law(cos_coef, sin_coef, harms)
            flat = jnp.concatenate(
                [jnp.concatenate(cos_out, axis=0), jnp.concatenate(sin_out, axis=0)], axis=1
            )
            high, middle, low = split3(flat)
            p = perm_t[...]
            rows = dot(high, p) + (dot(middle, p) + dot(low, p))
            for k in range(harms):
                for n in range(nch):
                    place = pl.ds(pl.multiple_of((i + n * strips) * 8, 8), 8)
                    oc[r][c][k, place, :] = rows[8 * k : 8 * k + 8, n * width : (n + 1) * width]

    chunks = range(nch)
    lanes = [pl.ds(c * width, width) for c in chunks]
    halves = width // 128

    for c in chunks:
        send_blocks(0, c, ld)

    for r in range(ROUNDS):
        source = ld if r == 0 else tr
        sums = {}
        for c in chunks:
            square = difference(2 * r, c, source, jj)
            product(c, im)
            send_blocks(2 * r + 1, c, im)
            sums[c] = [square, inner(c, jj, im)]
        for c in chunks:
            square = difference(2 * r + 1, c, im, dv)
            product(c, gg)
            sums[c] += [square, inner(c, dv, gg)]
            for n in range(halves):
                for i in range(4):
                    piece = sums[c][i][:, n * 128 : (n + 1) * 128]
                    sum_y[r][c][my_y, pl.ds(4 * n + i, 1), :] = piece
            for d in range(1, NY):
                y_copy(r, c, d).start()
        for c in chunks:
            for d in range(1, NY):
                y_copy(r, c, d).wait_recv()
            total = sum_y[r][c][0]
            for d in range(1, NY):
                total = total + sum_y[r][c][d]
            sum_z[r][c][my_z] = total
            for d in z_order:
                z_copy(r, c, d).start()
        for c in chunks:
            for d in z_order:
                z_copy(r, c, d).wait_recv()
            total = jnp.sum(sum_z[r][c][...], axis=0)
            square, curve, square_d, curve_d = [
                jnp.concatenate([total[4 * n + i : 4 * n + i + 1] for n in range(halves)], axis=1)
                for i in range(4)
            ]
            first = square / (curve + TINY)
            square = square - 4.0 * first * curve + first * first * square_d
            curve = curve - first * square_d + first * first * curve_d
            second = square / (curve + TINY)
            both, cross = first + second, first * second
            for q in range(CB):
                b = cblk[0, q]
                value = source[c, b] - both * im[c, b] + cross * gg[c, b]
                ct[r][c][pl.ds(q * BLK, BLK), :] = value
            for d in h_order:
                to_harm(r, c, d).start()
            rc[r][c][harm] = ct[r][c][rows_of(harm), :]

            @pl.loop(0, NB)
            def _(b):
                change = cross * dv[c, b] - both * jj[c, b]
                mm[c, b] = change if r == 0 else mm[c, b] + change
                if r + 1 < ROUNDS:
                    tr[c, b] = source[c, b] - both * im[c, b] + cross * gg[c, b]

        for c in chunks:
            for d in h_order:
                to_harm(r, c, d).wait_recv()
            contact(r, c)
            for d in h_order:
                from_harm(r, c, d).start()
            bc[r][c][rows_of(harm), :] = oc[r][c][harm]
        for c in chunks:
            for d in h_order:
                from_harm(r, c, d).wait_recv()
            for q in range(CB):
                rows = pl.ds(q * BLK, BLK)
                cf[c, q] = bc[r][c][rows, :] * stc[rows, :]

            @pl.loop(0, NB)
            def _(b):
                value = jnp.where(tab[3, b] != 0, cf[c, tab[2, b]], 0.0)
                mm[c, b] = mm[c, b] - value
                if r + 1 < ROUNDS:
                    xh[c, b], xl[c, b] = split(value)

            if r + 1 < ROUNDS:
                product(c, tr, subtract=True)
                send_blocks(2 * r + 2, c, tr)
            else:
                pltpu.make_async_copy(mm.at[c], mult.at[:, :, lanes[c]], out_sem.at[c, 0]).start()
                pltpu.make_async_copy(cf.at[c], force.at[:, :, lanes[c]], out_sem.at[c, 1]).start()

    for c in chunks:
        for r in range(ROUNDS):
            for way in range(2):
                exchange(2 * r, c, way).wait_send()
                exchange(2 * r + 1, c, way).wait_send()
            for d in range(1, NY):
                y_copy(r, c, d).wait_send()
            for d in z_order:
                z_copy(r, c, d).wait_send()
            for d in h_order:
                to_harm(r, c, d).wait_send()
                from_harm(r, c, d).wait_send()
        pltpu.make_async_copy(mm.at[c], mult.at[:, :, lanes[c]], out_sem.at[c, 0]).wait()
        pltpu.make_async_copy(cf.at[c], force.at[:, :, lanes[c]], out_sem.at[c, 1]).wait()


def per_device(flex, loads, side, partner, contact_blocks, contact_stiff):
    harms = lax.axis_size("harm")
    nz = lax.axis_size("sub") // NY
    nch = CHUNKS
    width = COLS // nch
    part = CROWS // harms
    sums = 4 * (width // 128)
    field = pltpu.VMEM((nch, NB, BLK, width), f32)
    field16 = pltpu.VMEM((nch, NB, BLK, width), bf16)
    scratch = [
        pltpu.VMEM((ROWS, ROWS), f32),
        pltpu.VMEM((ROWS, ROWS), bf16),
        pltpu.VMEM((ROWS, ROWS), bf16),
    ]
    scratch += [field] * 7 + [field16] * 2
    scratch += [
        pltpu.VMEM((nch, CB, BLK, width), f32),
        pltpu.VMEM((CROWS, width), f32),
        pltpu.VMEM((COLS, COLS), bf16),
        pltpu.VMEM((COLS, COLS), bf16),
        pltpu.SMEM((5, NB), jnp.int32),
    ]
    grid = lambda n, shape: [pltpu.VMEM(shape, f32)] * (n * nch)
    scratch += grid(2 * ROUNDS, (2 * MAXB, BLK, width)) * 2
    scratch += grid(ROUNDS, (NY, sums, 128)) + grid(ROUNDS, (nz, sums, 128))
    scratch += grid(ROUNDS, (CROWS, width)) + grid(ROUNDS, (harms, part, width)) * 2
    scratch += grid(ROUNDS, (CROWS, width))
    sem = pltpu.SemaphoreType.DMA
    scratch += [sem((nch + 1,)), sem((nch, 2))]
    scratch += [sem((2 * ROUNDS, nch, 2))] * 2
    scratch += [sem((ROUNDS, nch, NY))] * 2
    scratch += [sem((ROUNDS, nch, nz))] * 2
    scratch += [sem((ROUNDS, nch, 2, harms))] * 2
    smem = pl.BlockSpec(memory_space=pltpu.SMEM)
    anywhere = pl.BlockSpec(memory_space=pl.ANY)
    mult, force = pl.pallas_call(
        functools.partial(kernel, nz, harms),
        out_shape=(
            jax.ShapeDtypeStruct((NB, BLK, COLS), f32),
            jax.ShapeDtypeStruct((CB, BLK, COLS), f32),
        ),
        in_specs=[smem] * 3 + [pl.BlockSpec(memory_space=pltpu.VMEM)] + [anywhere] * 2,
        out_specs=(anywhere, anywhere),
        scratch_shapes=scratch,
        compiler_params=pltpu.CompilerParams(
            collective_id=0, has_side_effects=True, vmem_limit_bytes=48 << 20
        ),
    )(
        side,
        partner,
        contact_blocks,
        contact_stiff,
        flex.reshape(ROWS, ROWS),
        loads.reshape(NB, BLK, COLS),
    )
    return mult.reshape(loads.shape), force.reshape(1, 1, CROWS, COLS)


def solution(mesh):
    return jax.shard_map(
        per_device,
        mesh=mesh,
        in_specs=(
            P("sub", "harm", None, None),
            P("sub", "harm", None, None),
            P("sub", None),
            P("sub", None),
            P("sub", None),
            P("sub", None),
        ),
        out_specs=(P("sub", "harm", None, None), P("sub", "harm", None, None)),
        check_vma=False,
    )
```

```python
import functools
import math

import jax
import jax.numpy as jnp
from jax import lax
from jax.experimental import pallas as pl
from jax.experimental.pallas import tpu as pltpu
from jax.sharding import PartitionSpec as P

MESH = pl.DeviceIdType.MESH
TIMES = 64
ROUNDS = 2
TINY = 1e-6
NB = 12
BLK = 64
ROWS = NB * BLK
COLS = 256
MAXB = 4
CB = 4
CROWS = CB * BLK
NY = 4
NCH = 2
WIDTH = COLS // NCH
S_ROWS = 2 * MAXB * BLK
TILE = 256
PAIRS = ROWS // 128
OUT = pl.BlockSpec(memory_space=pltpu.VMEM)

f32 = jnp.float32
bf16 = jnp.bfloat16


def dot(a, b):
    return jnp.dot(a, b, preferred_element_type=f32)


def split(x):
    high = x.astype(bf16)
    return high, (x - high.astype(f32)).astype(bf16)


def cube_law(coefs, table, odd_lane):
    harms = len(coefs)
    out = [None] * harms

    def plus(x, y):
        return y if x is None else x + y

    def cubes(y):
        square = y * y
        turned = pltpu.roll(square, 127, axis=2), pltpu.roll(square, 1, axis=2)
        return y * (square + 3.0 * jnp.where(odd_lane, turned[1], turned[0]))

    for t in range(TIMES // 4 + 1):
        parity = [None, None]
        for k in range(harms):
            parity[(k + 1) % 2] = plus(parity[(k + 1) % 2], coefs[k] * table[t, k])
        first, second = cubes(parity[0] + parity[1]), cubes(parity[0] - parity[1])
        both = [first + second, first - second]
        if t in (0, TIMES // 4):
            both = [0.5 * x for x in both]
        for k in range(harms):
            out[k] = plus(out[k], both[(k + 1) % 2] * table[t, k])
    return [(4.0 / TIMES) * x for x in out]


def relay_steps(nz):
    radius, steps = min(2, nz // 2), []
    while radius < nz // 2:
        steps.append(radius)
        radius *= 2
    return steps


def drain(ref, sem):
    pltpu.make_async_copy(ref, ref, sem).wait()


def signal(sem, peer):
    pl.semaphore_signal(sem, inc=1, device_id=peer, device_id_type=MESH)


def kernel(nz, harms, side_h, partner_h, cblk_h, stiff_h, flex_h, loads_h, mult, force, *scratch):
    names = iter(scratch)
    take = lambda n: [next(names) for _ in range(n)]
    side, partner, cblk, tab = take(4)
    stiff, flex, loads, fh, fl, x2, stc, waves = take(8)
    js, ds, gs, tn, ms = (take(NCH) for _ in range(5))
    imc, gc, tc, old, mo = (take(NCH) for _ in range(5))
    snd = [take(NCH) for _ in range(2 * ROUNDS)]
    rcv = [take(NCH) for _ in range(2 * ROUNDS)]
    sum_y, sum_z, ct, rc, oc, bc = ([take(NCH) for _ in range(ROUNDS)] for _ in range(6))
    in_sem, ex_s, ex_r, y_s, y_r, z_s, z_r, a_s, a_r = take(9)
    told = take(len(relay_steps(nz)))

    part = CROWS // harms
    sub = lax.axis_index("sub")
    harm = lax.axis_index("harm")
    subs = nz * NY
    my_y = lax.rem(sub, NY)
    my_z = sub // NY
    right = (lax.rem(sub + 1, subs), harm)
    left = (lax.rem(sub + subs - 1, subs), harm)
    y_peers = [(my_z * NY + lax.rem(my_y + d, NY), harm) for d in range(1, NY)]
    z_order = sorted(range(1, nz), key=lambda d: -min(d, nz - d))
    z_peers = {d: (lax.rem(my_z + d, nz) * NY + my_y, harm) for d in z_order}
    h_order = sorted(range(1, harms), key=lambda d: -min(d, harms - d))
    h_peers = {d: lax.rem(harm + d, harms) for d in h_order}

    copies = [
        pltpu.make_async_copy(one, two, in_sem.at[i])
        for i, (one, two) in enumerate(
            (
                (side_h, side),
                (partner_h, partner),
                (cblk_h, cblk),
                (loads_h, loads),
                (stiff_h, stiff),
            )
        )
    ]
    copies += [
        pltpu.make_async_copy(
            flex_h.at[:, :, pl.ds(128 * i, 128)], flex.at[i], in_sem.at[len(copies)]
        )
        for i in range(PAIRS)
    ]
    for copy in copies[:3]:
        copy.start()
    barrier = pltpu.get_barrier_semaphore()
    near = [d for d in z_order if min(d, nz - d) <= 2]
    greet = [right, left] + [z_peers[d] for d in near] + y_peers + [(sub, h_peers[d]) for d in h_order]
    for peer in greet:
        signal(barrier, peer)

    for copy in copies[3:]:
        copy.start()
    for copy in copies[:3]:
        copy.wait()

    sides = [side[0, b] for b in range(NB)]
    partners = [partner[0, b] for b in range(NB)]
    contacts = [cblk[0, q] for q in range(CB)]
    one, zero = jnp.int32(1), jnp.int32(0)
    ranks = []
    count_r = count_l = zero
    for b in range(NB):
        rank = zero
        for other in range(NB):
            if other != b:
                before = (sides[other] == -1) & (partners[other] < partners[b])
                rank = rank + jnp.where(before, one, zero)
        is_r, is_l = sides[b] == 1, sides[b] == -1
        slot = jnp.where(is_r, count_r, jnp.where(is_l, MAXB + rank, zero))
        slot = jnp.minimum(slot, 2 * MAXB - 1)
        count_r = count_r + jnp.where(is_r, one, zero)
        count_l = count_l + jnp.where(is_l, one, zero)
        ranks.append(jnp.where(sides[b] != 0, slot, -1))
        tab[2, b] = slot
        tab[3, b] = jnp.where(sides[b] != 0, one, zero)
    for k in range(2 * MAXB):
        block = zero
        for b in range(NB):
            block = jnp.where(ranks[b] == k, b, block)
        tab[0, k] = block
        tab[1, k] = jnp.where(k % MAXB < (count_r if k < MAXB else count_l), one, zero)
    for q in range(CB):
        tab[0, 2 * MAXB + q] = contacts[q]
    def exchange(e, c, way):
        return pltpu.make_async_remote_copy(
            src_ref=snd[e][c].at[pl.ds(way * MAXB, MAXB)],
            dst_ref=rcv[e][c].at[pl.ds((1 - way) * MAXB, MAXB)],
            send_sem=ex_s.at[e, c],
            recv_sem=ex_r.at[e, c],
            device_id=right if way == 0 else left,
            device_id_type=MESH,
        )

    def tell(i):
        steps = relay_steps(nz)
        if i < len(steps):
            signal(told[i], z_peers[steps[i]])
            signal(told[i], z_peers[nz - steps[i]])

    def hear(i):
        if i < len(told):
            pl.semaphore_wait(told[i], 2)
            tell(i + 1)

    def send(e, c):
        for way in range(2):
            exchange(e, c, way).start()

    copies[3].wait()
    lanes = [pl.ds(c * WIDTH, WIDTH) for c in range(NCH)]

    for c in range(NCH):

        @pl.loop(0, 2 * MAXB)
        def _(k):
            snd[0][c][k] = loads[tab[0, k], :, lanes[c]]

    pl.semaphore_wait(barrier, len(greet))
    send(0, 0)
    tell(0)

    for b in range(NB):
        place = found = zero
        for q in range(CB):
            same = contacts[q] == b
            place = jnp.where(same, q, place)
            found = jnp.where(same, one, found)
        tab[4, b] = place
        tab[5, b] = found

    for c in range(NCH):
        for q in range(CB):
            tc[c][q] = loads[cblk[0, q], :, lanes[c]]

    drain(flex, in_sem.at[5])
    lane = lax.broadcasted_iota(jnp.int32, (BLK, 128), 1)

    @pl.loop(0, 2 * MAXB + CB)
    def _(k):
        place = pl.ds(pl.multiple_of(k * BLK, BLK), BLK)

        def half(block, odd):
            pair = lax.div(block, jnp.int32(2))
            value = flex[pair, tab[0, k]]
            turned = pltpu.roll(value, 64, axis=1)
            return jnp.where(block - 2 * pair == odd, value, turned)

        for i in range(PAIRS):
            value = jnp.where(lane < 64, half(tab[0, 2 * i], 0), half(tab[0, 2 * i + 1], 1))
            cols = slice(128 * i, 128 * i + 128)
            fh[place, cols], fl[place, cols] = split(value)

    hear(0)
    drain(snd[0][0], ex_s.at[0, 0])
    send(0, 1)

    odd_lane = lax.broadcasted_iota(jnp.int32, (8, 128), 1) % 2 == 1
    for t in range(TIMES // 4 + 1):
        for k in range(harms):
            angle = 2 * math.pi * t * (k + 1) / TIMES
            waves[t, k] = jnp.where(odd_lane, math.sin(angle), math.cos(angle)).astype(f32)
    copies[4].wait()
    row = lax.broadcasted_iota(jnp.int32, (CROWS, CROWS), 0)
    col = lax.broadcasted_iota(jnp.int32, (CROWS, CROWS), 1)
    column = jnp.sum(jnp.where(row == col, stiff[...], 0.0), axis=1, keepdims=True)
    stc[...] = jnp.broadcast_to(column, (CROWS, WIDTH))

    def fold(x):
        return jnp.sum(x.reshape(BLK // 8, 8, WIDTH), axis=0)

    def put(k, value):
        rows = pl.ds(pl.multiple_of(k * BLK, BLK), BLK)
        x2[rows, :WIDTH], x2[rows, WIDTH:] = split(value)

    def total(acc):
        return jnp.sum(acc, axis=0, keepdims=True)

    def difference(e, c, target):
        def step(k, acc):
            value = snd[e][c][k] - rcv[e][c][k]
            value = jnp.where(tab[1, k] != 0, value, 0.0)
            target[k] = value
            put(k, value)
            return acc + fold(value * value)

        return total(lax.fori_loop(0, 2 * MAXB, step, jnp.zeros((8, WIDTH), f32)))

    def inner(one, two):
        acc = jnp.zeros((8, WIDTH), f32)
        return total(lax.fori_loop(0, 2 * MAXB, lambda k, a: a + fold(one[k] * two[k]), acc))

    def product(rows, cols, target, base=None):
        x = x2[0 : cols[1] - cols[0], :]
        for at in range(rows[0], rows[1], TILE):
            first = fh[at : at + TILE, cols[0] : cols[1]]
            second = fl[at : at + TILE, cols[0] : cols[1]]
            out = dot(first, x) + dot(second, x)
            out = (out[:, :WIDTH] + out[:, WIDTH:]).reshape(TILE // BLK, BLK, WIDTH)
            blocks = pl.ds((at - rows[0]) // BLK, TILE // BLK)
            target[blocks] = out if base is None else base[blocks] - out

    def y_copy(r, c, d):
        ref = sum_y[r][c].at[my_y]
        return pltpu.make_async_remote_copy(
            src_ref=ref,
            dst_ref=ref,
            send_sem=y_s.at[r, c],
            recv_sem=y_r.at[r, c],
            device_id=y_peers[d - 1],
            device_id_type=MESH,
        )

    def z_copy(r, c, d):
        ref = sum_z[r][c].at[my_z]
        return pltpu.make_async_remote_copy(
            src_ref=ref,
            dst_ref=ref,
            send_sem=z_s.at[r, c],
            recv_sem=z_r.at[r, c],
            device_id=z_peers[d],
            device_id_type=MESH,
        )

    def rows_of(index):
        return pl.ds(pl.multiple_of(index * part, part), part)

    def to_harm(r, c, d):
        return pltpu.make_async_remote_copy(
            src_ref=ct[r][c].at[rows_of(h_peers[d])],
            dst_ref=rc[r][c].at[harm],
            send_sem=a_s.at[r, c, 0],
            recv_sem=a_r.at[r, c, 0],
            device_id=(sub, h_peers[d]),
            device_id_type=MESH,
        )

    def from_harm(r, c, d):
        return pltpu.make_async_remote_copy(
            src_ref=oc[r][c].at[h_peers[d]],
            dst_ref=bc[r][c].at[rows_of(harm)],
            send_sem=a_s.at[r, c, 1],
            recv_sem=a_r.at[r, c, 1],
            device_id=(sub, h_peers[d]),
            device_id_type=MESH,
        )

    def contact(r, c):
        odd = jnp.broadcast_to(odd_lane, (2, 8, 128))

        @pl.loop(0, part // 16)
        def _(i):
            rows = pl.ds(pl.multiple_of(i * 16, 16), 16)
            coefs = [rc[r][c][k, rows, :].reshape(2, 8, 128) for k in range(harms)]
            for k, value in enumerate(cube_law(coefs, waves, odd)):
                oc[r][c][k, rows, :] = value.reshape(16, 128)

    shared, joint, every = (0, S_ROWS), (S_ROWS, ROWS), range(NCH)

    def stage_jump(r, c):
        drain(rcv[2 * r][c], ex_r.at[2 * r, c])
        square = difference(2 * r, c, js[c])
        product(shared, shared, snd[2 * r + 1][c])
        send(2 * r + 1, c)
        product(joint, shared, imc[c])
        sum_z[r][c][my_z, 0:1, :] = square
        sum_z[r][c][my_z, 1:2, :] = inner(js[c], snd[2 * r + 1][c])

    def stage_image(r, c):
        drain(rcv[2 * r + 1][c], ex_r.at[2 * r + 1, c])
        square = difference(2 * r + 1, c, ds[c])
        product(shared, shared, gs[c])
        sum_z[r][c][my_z, 2:3, :] = square
        sum_z[r][c][my_z, 3:4, :] = inner(ds[c], gs[c])
        if r == 0 and c == 0:
            hear(1)
            assert len(told) <= 2
        for d in z_order:
            z_copy(r, c, d).start()
        product(joint, shared, gc[c])

    def stage_sums(r, c):
        drain(sum_z[r][c].at[pl.ds(0, nz - 1)], z_r.at[r, c])
        sum_y[r][c][my_y] = jnp.sum(sum_z[r][c][...], axis=0)
        for d in range(1, NY):
            y_copy(r, c, d).start()

    def stage_step(r, c):
        drain(sum_y[r][c].at[pl.ds(0, NY - 1)], y_r.at[r, c])
        value = jnp.sum(sum_y[r][c][...], axis=0)
        square, curve, square_d, curve_d = (value[i : i + 1] for i in range(4))
        first = square / (curve + TINY)
        square = square - 4.0 * first * curve + first * first * square_d
        curve = curve - first * square_d + first * first * curve_d
        second = square / (curve + TINY)
        both, cross = first + second, first * second
        for q in range(CB):
            value = tc[c][q] - both * imc[c][q] + cross * gc[c][q]
            ct[r][c][pl.ds(q * BLK, BLK), :] = value
        for d in h_order:
            to_harm(r, c, d).start()
        rc[r][c][harm] = ct[r][c][rows_of(harm), :]

        @pl.loop(0, 2 * MAXB)
        def _(k):
            change = cross * ds[c][k] - both * js[c][k]
            ms[c][k] = change if r == 0 else ms[c][k] + change
            if r + 1 < ROUNDS:
                image = snd[2 * r + 1][c][k]
                tn[c][k] = snd[2 * r][c][k] - both * image + cross * gs[c][k]

        if r + 1 == ROUNDS:

            @pl.loop(0, NB)
            def _(b):
                value = jnp.where(tab[3, b] != 0, ms[c][tab[2, b]], 0.0)
                mo[c][b] = value - jnp.where(tab[5, b] != 0, old[c][tab[4, b]], 0.0)

    def stage_contact(r, c):
        drain(rc[r][c].at[pl.ds(0, harms - 1)], a_r.at[r, c, 0])
        contact(r, c)
        for d in h_order:
            from_harm(r, c, d).start()
        bc[r][c][rows_of(harm), :] = oc[r][c][harm]

    def stage_force(r, c):
        drain(bc[r][c].at[pl.ds(0, (harms - 1) * part)], a_r.at[r, c, 1])
        for q in range(CB):
            rows = pl.ds(q * BLK, BLK)
            value = bc[r][c][rows, :] * stc[rows, :]
            if r + 1 < ROUNDS:
                old[c][q] = value
                put(q, value)
            else:
                old[c][q] = value
                force[q, :, lanes[c]] = value
        if r + 1 < ROUNDS:
            product(shared, joint, snd[2 * r + 2][c], tn[c])
            send(2 * r + 2, c)
            for q in range(CB):
                tc[c][q] = ct[r][c][pl.ds(q * BLK, BLK), :]
            product(joint, joint, tc[c], tc[c])
        else:

            @pl.loop(0, NB)
            def _(b):
                value = jnp.where(tab[5, b] != 0, old[c][tab[4, b]], 0.0)
                mult[b, :, lanes[c]] = mo[c][b] - value

    def settle(r, c):
        if r > 0 or c > 0:
            drain(snd[2 * r][c], ex_s.at[2 * r, c])
        drain(snd[2 * r + 1][c], ex_s.at[2 * r + 1, c])
        drain(sum_y[r][c].at[pl.ds(0, NY - 1)], y_s.at[r, c])
        drain(sum_z[r][c].at[pl.ds(0, nz - 1)], z_s.at[r, c])
        drain(ct[r][c].at[pl.ds(0, (harms - 1) * part)], a_s.at[r, c, 0])

    def settle_last(r, c):
        drain(oc[r][c].at[pl.ds(0, harms - 1)], a_s.at[r, c, 1])

    for r in range(ROUNDS):
        for c in every:
            stage_jump(r, c)
            if r > 0 and c == NCH - 1:
                for old_c in every:
                    settle(r - 1, old_c)
                    settle_last(r - 1, old_c)
        for c in every:
            stage_image(r, c)
        for c in every:
            stage_sums(r, c)
            if c > 0:
                stage_step(r, c - 1)
        stage_step(r, NCH - 1)
        for c in every:
            stage_contact(r, c)
        if r == ROUNDS - 1:
            for c in every:
                settle(r, c)
        for c in every:
            stage_force(r, c)
    for c in every:
        settle_last(ROUNDS - 1, c)


def per_device(flex, loads, side, partner, contact_blocks, contact_stiff):
    harms = lax.axis_size("harm")
    nz = lax.axis_size("sub") // NY
    part = CROWS // harms
    slots, joint, whole = (
        [pltpu.VMEM((n, BLK, WIDTH), f32)] * NCH for n in (2 * MAXB, CB, NB)
    )
    vmem = lambda *shape: [pltpu.VMEM(shape, f32)] * (NCH * ROUNDS)
    sem = pltpu.SemaphoreType.DMA
    scratch = [
        pltpu.SMEM((1, NB), jnp.int32),
        pltpu.SMEM((1, NB), jnp.int32),
        pltpu.SMEM((1, CB), jnp.int32),
        pltpu.SMEM((6, NB), jnp.int32),
        pltpu.VMEM((1, CROWS), f32),
        pltpu.VMEM((PAIRS, NB, BLK, 128), f32),
        pltpu.VMEM((NB, BLK, COLS), f32),
        pltpu.VMEM((ROWS, ROWS), bf16),
        pltpu.VMEM((ROWS, ROWS), bf16),
        pltpu.VMEM((S_ROWS, 2 * WIDTH), bf16),
        pltpu.VMEM((CROWS, WIDTH), f32),
        pltpu.VMEM((TIMES // 4 + 1, harms, 8, 128), f32),
    ]
    scratch += slots * 5 + joint * 4 + whole
    scratch += slots * (2 * ROUNDS) * 2
    scratch += vmem(NY, 4, WIDTH) + vmem(nz, 4, WIDTH)
    scratch += vmem(CROWS, WIDTH) + vmem(harms, part, WIDTH) * 2 + vmem(CROWS, WIDTH)
    scratch += [sem((6,))]
    scratch += [sem((2 * ROUNDS, NCH))] * 2
    scratch += [sem((ROUNDS, NCH))] * 4
    scratch += [sem((ROUNDS, NCH, 2))] * 2
    scratch += [pltpu.SemaphoreType.REGULAR] * len(relay_steps(nz))
    hbm = pl.BlockSpec(memory_space=pltpu.HBM)
    mult, force = pl.pallas_call(
        functools.partial(kernel, nz, harms),
        out_shape=(
            jax.ShapeDtypeStruct((NB, BLK, COLS), f32),
            jax.ShapeDtypeStruct((CB, BLK, COLS), f32),
        ),
        in_specs=[hbm] * 6,
        out_specs=(OUT, OUT),
        scratch_shapes=scratch,
        compiler_params=pltpu.CompilerParams(
            collective_id=0, has_side_effects=True, vmem_limit_bytes=48 << 20
        ),
    )(
        *(
            pltpu.with_memory_space_constraint(x, pltpu.HBM)
            for x in (
                side,
                partner,
                contact_blocks,
                contact_stiff,
                flex.reshape(NB, BLK, ROWS),
                loads.reshape(NB, BLK, COLS),
            )
        )
    )
    return mult.reshape(loads.shape), force.reshape(1, 1, CROWS, COLS)


def solution(mesh):
    return jax.shard_map(
        per_device,
        mesh=mesh,
        in_specs=(
            P("sub", "harm", None, None),
            P("sub", "harm", None, None),
            P("sub", None),
            P("sub", None),
            P("sub", None),
            P("sub", None),
        ),
        out_specs=(P("sub", "harm", None, None), P("sub", "harm", None, None)),
        check_vma=False,
    )
```

```python
import functools
import math

import jax
import jax.numpy as jnp
from jax import lax
from jax.experimental import pallas as pl
from jax.experimental.pallas import tpu as pltpu
from jax.sharding import PartitionSpec as P

MESH = pl.DeviceIdType.MESH
TIMES = 64
ROUNDS = 2
TINY = 1e-6
NB = 12
BLK = 64
ROWS = NB * BLK
COLS = 256
MAXB = 4
CB = 4
CROWS = CB * BLK
NY = 4
NCH = 2
WIDTH = COLS // NCH
S_ROWS = 2 * MAXB * BLK
TILE = 256
PAIRS = ROWS // 128
OUT = pl.BlockSpec(memory_space=pltpu.VMEM)

f32 = jnp.float32
bf16 = jnp.bfloat16


def dot(a, b):
    return jnp.dot(a, b, preferred_element_type=f32)


def split(x):
    high = x.astype(bf16)
    return high, (x - high.astype(f32)).astype(bf16)


def cube_law(coefs, table, odd_lane):
    harms = len(coefs)
    out = [None] * harms

    def plus(x, y):
        return y if x is None else x + y

    def cubes(y):
        square = y * y
        turned = pltpu.roll(square, 127, axis=2), pltpu.roll(square, 1, axis=2)
        return y * (square + 3.0 * jnp.where(odd_lane, turned[1], turned[0]))

    for t in range(TIMES // 4 + 1):
        parity = [None, None]
        for k in range(harms):
            parity[(k + 1) % 2] = plus(parity[(k + 1) % 2], coefs[k] * table[t, k])
        first, second = cubes(parity[0] + parity[1]), cubes(parity[0] - parity[1])
        both = [first + second, first - second]
        if t in (0, TIMES // 4):
            both = [0.5 * x for x in both]
        for k in range(harms):
            out[k] = plus(out[k], both[(k + 1) % 2] * table[t, k])
    return [(4.0 / TIMES) * x for x in out]


def relay_steps(nz):
    radius, steps = min(2, nz // 2), []
    while radius < nz // 2:
        steps.append(radius)
        radius *= 2
    return steps


def drain(ref, sem):
    pltpu.make_async_copy(ref, ref, sem).wait()


def signal(sem, peer):
    pl.semaphore_signal(sem, inc=1, device_id=peer, device_id_type=MESH)


def kernel(nz, harms, side_h, partner_h, cblk_h, stiff_h, flex_h, loads_h, mult, force, *scratch):
    names = iter(scratch)
    take = lambda n: [next(names) for _ in range(n)]
    side, partner, cblk, tab = take(4)
    stiff, flex, loads, fh, fl, x2, stc, waves = take(8)
    js, ds, gs, tn, ms = (take(NCH) for _ in range(5))
    steps, old, mo = (take(NCH) for _ in range(3))
    snd = [take(NCH) for _ in range(2 * ROUNDS)]
    rcv = [take(NCH) for _ in range(2 * ROUNDS)]
    sum_z, sum_y, oc, bc = ([take(NCH) for _ in range(ROUNDS)] for _ in range(4))
    mine = [[take(3) for _ in range(NCH)] for _ in range(ROUNDS)]
    all_of = [[take(3) for _ in range(NCH)] for _ in range(ROUNDS)]
    in_sem, ex_s, ex_r, y_s, y_r, z_s, z_r, a_s, a_r = take(9)
    told = take(len(relay_steps(nz)))

    part = CROWS // harms
    sub = lax.axis_index("sub")
    harm = lax.axis_index("harm")
    subs = nz * NY
    my_y = lax.rem(sub, NY)
    my_z = sub // NY
    right = (lax.rem(sub + 1, subs), harm)
    left = (lax.rem(sub + subs - 1, subs), harm)
    y_peers = [(my_z * NY + lax.rem(my_y + d, NY), harm) for d in range(1, NY)]
    pairs = [(d, h) for d in range(NY) for h in range(harms) if d + h > 0]
    pairs.sort(key=lambda p: -min(p[0], NY - p[0]) - min(p[1], harms - p[1]) / 2)
    plane_peers = [
        (my_z * NY + lax.rem(my_y + d, NY), lax.rem(harm + h, harms)) for d, h in pairs
    ]
    z_order = sorted(range(1, nz), key=lambda d: -min(d, nz - d))
    z_peers = {d: (lax.rem(my_z + d, nz) * NY + my_y, harm) for d in z_order}
    h_order = sorted(range(1, harms), key=lambda d: -min(d, harms - d))
    h_peers = {d: lax.rem(harm + d, harms) for d in h_order}

    copies = [
        pltpu.make_async_copy(one, two, in_sem.at[i])
        for i, (one, two) in enumerate(
            (
                (side_h, side),
                (partner_h, partner),
                (cblk_h, cblk),
                (loads_h, loads),
                (stiff_h, stiff),
            )
        )
    ]
    copies += [
        pltpu.make_async_copy(
            flex_h.at[:, :, pl.ds(128 * i, 128)], flex.at[i], in_sem.at[len(copies)]
        )
        for i in range(PAIRS)
    ]
    for copy in copies[:3]:
        copy.start()
    barrier = pltpu.get_barrier_semaphore()
    near = [d for d in z_order if min(d, nz - d) <= 2]
    greet = [right, left] + [z_peers[d] for d in near] + y_peers + [(sub, h_peers[d]) for d in h_order]
    for peer in greet:
        signal(barrier, peer)

    for copy in copies[3:]:
        copy.start()
    for copy in copies[:3]:
        copy.wait()

    sides = [side[0, b] for b in range(NB)]
    partners = [partner[0, b] for b in range(NB)]
    contacts = [cblk[0, q] for q in range(CB)]
    one, zero = jnp.int32(1), jnp.int32(0)
    ranks = []
    count_r = count_l = zero
    for b in range(NB):
        rank = zero
        for other in range(NB):
            if other != b:
                before = (sides[other] == -1) & (partners[other] < partners[b])
                rank = rank + jnp.where(before, one, zero)
        is_r, is_l = sides[b] == 1, sides[b] == -1
        slot = jnp.where(is_r, count_r, jnp.where(is_l, MAXB + rank, zero))
        slot = jnp.minimum(slot, 2 * MAXB - 1)
        count_r = count_r + jnp.where(is_r, one, zero)
        count_l = count_l + jnp.where(is_l, one, zero)
        ranks.append(jnp.where(sides[b] != 0, slot, -1))
        tab[2, b] = slot
        tab[3, b] = jnp.where(sides[b] != 0, one, zero)
    for k in range(2 * MAXB):
        block = zero
        for b in range(NB):
            block = jnp.where(ranks[b] == k, b, block)
        tab[0, k] = block
        tab[1, k] = jnp.where(k % MAXB < (count_r if k < MAXB else count_l), one, zero)
    for q in range(CB):
        tab[0, 2 * MAXB + q] = contacts[q]
    def exchange(e, c, way):
        return pltpu.make_async_remote_copy(
            src_ref=snd[e][c].at[pl.ds(way * MAXB, MAXB)],
            dst_ref=rcv[e][c].at[pl.ds((1 - way) * MAXB, MAXB)],
            send_sem=ex_s.at[e, c],
            recv_sem=ex_r.at[e, c],
            device_id=right if way == 0 else left,
            device_id_type=MESH,
        )

    def tell(i):
        steps = relay_steps(nz)
        if i < len(steps):
            signal(told[i], z_peers[steps[i]])
            signal(told[i], z_peers[nz - steps[i]])

    def hear(i):
        if i < len(told):
            pl.semaphore_wait(told[i], 2)
            tell(i + 1)

    def send(e, c):
        for way in range(2):
            exchange(e, c, way).start()

    copies[3].wait()
    lanes = [pl.ds(c * WIDTH, WIDTH) for c in range(NCH)]

    for c in range(NCH):

        @pl.loop(0, 2 * MAXB)
        def _(k):
            snd[0][c][k] = loads[tab[0, k], :, lanes[c]]

    pl.semaphore_wait(barrier, len(greet))
    send(0, 0)
    tell(0)

    for b in range(NB):
        place = found = zero
        for q in range(CB):
            same = contacts[q] == b
            place = jnp.where(same, q, place)
            found = jnp.where(same, one, found)
        tab[4, b] = place
        tab[5, b] = found

    def rows_of(index):
        return pl.ds(pl.multiple_of(index * part, part), part)

    def to_harm(r, c, i, d):
        return pltpu.make_async_remote_copy(
            src_ref=mine[r][c][i].at[rows_of(h_peers[d])],
            dst_ref=all_of[r][c][i].at[harm],
            send_sem=a_s.at[r, c, i],
            recv_sem=a_r.at[r, c, i],
            device_id=(sub, h_peers[d]),
            device_id_type=MESH,
        )

    def share(r, c, i):
        for d in h_order:
            to_harm(r, c, i, d).start()
        all_of[r][c][i][harm] = mine[r][c][i][rows_of(harm), :]

    for c in range(NCH):
        for q in range(CB):
            mine[0][c][0][pl.ds(q * BLK, BLK), :] = loads[cblk[0, q], :, lanes[c]]
        share(0, c, 0)

    drain(flex, in_sem.at[5])
    lane = lax.broadcasted_iota(jnp.int32, (BLK, 128), 1)

    @pl.loop(0, 2 * MAXB + CB)
    def _(k):
        place = pl.ds(pl.multiple_of(k * BLK, BLK), BLK)

        def half(block, odd):
            pair = lax.div(block, jnp.int32(2))
            value = flex[pair, tab[0, k]]
            turned = pltpu.roll(value, 64, axis=1)
            return jnp.where(block - 2 * pair == odd, value, turned)

        for i in range(PAIRS):
            value = jnp.where(lane < 64, half(tab[0, 2 * i], 0), half(tab[0, 2 * i + 1], 1))
            cols = slice(128 * i, 128 * i + 128)
            fh[place, cols], fl[place, cols] = split(value)

    hear(0)
    drain(snd[0][0], ex_s.at[0, 0])
    send(0, 1)

    odd_lane = lax.broadcasted_iota(jnp.int32, (8, 128), 1) % 2 == 1
    for t in range(TIMES // 4 + 1):
        for k in range(harms):
            angle = 2 * math.pi * t * (k + 1) / TIMES
            waves[t, k] = jnp.where(odd_lane, math.sin(angle), math.cos(angle)).astype(f32)
    copies[4].wait()
    row = lax.broadcasted_iota(jnp.int32, (CROWS, CROWS), 0)
    col = lax.broadcasted_iota(jnp.int32, (CROWS, CROWS), 1)
    column = jnp.sum(jnp.where(row == col, stiff[...], 0.0), axis=1, keepdims=True)
    stc[...] = jnp.broadcast_to(column, (CROWS, WIDTH))

    def fold(x):
        return jnp.sum(x.reshape(BLK // 8, 8, WIDTH), axis=0)

    def put(k, value):
        rows = pl.ds(pl.multiple_of(k * BLK, BLK), BLK)
        x2[rows, :WIDTH], x2[rows, WIDTH:] = split(value)

    def total(acc):
        return jnp.sum(acc, axis=0, keepdims=True)

    def difference(e, c, target):
        def step(k, acc):
            value = snd[e][c][k] - rcv[e][c][k]
            value = jnp.where(tab[1, k] != 0, value, 0.0)
            target[k] = value
            put(k, value)
            return acc + fold(value * value)

        return total(lax.fori_loop(0, 2 * MAXB, step, jnp.zeros((8, WIDTH), f32)))

    def inner(one, two):
        acc = jnp.zeros((8, WIDTH), f32)
        return total(lax.fori_loop(0, 2 * MAXB, lambda k, a: a + fold(one[k] * two[k]), acc))

    def product(rows, cols, put_tile):
        x = x2[0 : cols[1] - cols[0], :]
        for at in range(rows[0], rows[1], TILE):
            first = fh[at : at + TILE, cols[0] : cols[1]]
            second = fl[at : at + TILE, cols[0] : cols[1]]
            out = dot(first, x) + dot(second, x)
            put_tile(at - rows[0], out[:, :WIDTH] + out[:, WIDTH:])

    def into_slots(target, base=None):
        def put_tile(at, out):
            blocks = pl.ds(at // BLK, TILE // BLK)
            out = out.reshape(TILE // BLK, BLK, WIDTH)
            target[blocks] = out if base is None else base[blocks] - out

        return put_tile

    def into_rows(target, base=None):
        def put_tile(at, out):
            rows = pl.ds(at, TILE)
            target[rows, :] = out if base is None else base[rows, :] - out

        return put_tile

    def y_copy(r, c, peer):
        ref = sum_y[r][c].at[my_y * harms + harm]
        return pltpu.make_async_remote_copy(
            src_ref=ref,
            dst_ref=ref,
            send_sem=y_s.at[r, c],
            recv_sem=y_r.at[r, c],
            device_id=peer,
            device_id_type=MESH,
        )

    def z_copy(r, c, d):
        ref = sum_z[r][c].at[my_z]
        return pltpu.make_async_remote_copy(
            src_ref=ref,
            dst_ref=ref,
            send_sem=z_s.at[r, c],
            recv_sem=z_r.at[r, c],
            device_id=z_peers[d],
            device_id_type=MESH,
        )

    def from_harm(r, c, d):
        return pltpu.make_async_remote_copy(
            src_ref=oc[r][c].at[h_peers[d]],
            dst_ref=bc[r][c].at[rows_of(harm)],
            send_sem=a_s.at[r, c, 3],
            recv_sem=a_r.at[r, c, 3],
            device_id=(sub, h_peers[d]),
            device_id_type=MESH,
        )

    def contact(r, c):
        odd = jnp.broadcast_to(odd_lane, (2, 8, 128))

        @pl.loop(0, part // 16)
        def _(i):
            rows = pl.ds(pl.multiple_of(i * 16, 16), 16)
            coefs = []
            for k in range(harms):
                trace, image, second = (
                    all_of[r][c][n][k, rows, :].reshape(2, 8, 128) for n in range(3)
                )
                coefs.append(trace - steps[c][0, k] * image + steps[c][1, k] * second)
            for k, value in enumerate(cube_law(coefs, waves, odd)):
                oc[r][c][k, rows, :] = value.reshape(16, 128)

    shared, joint, every = (0, S_ROWS), (S_ROWS, ROWS), range(NCH)

    def stage_jump(r, c):
        drain(rcv[2 * r][c], ex_r.at[2 * r, c])
        square = difference(2 * r, c, js[c])
        product(shared, shared, into_slots(snd[2 * r + 1][c]))
        send(2 * r + 1, c)
        product(joint, shared, into_rows(mine[r][c][1]))
        share(r, c, 1)
        sum_z[r][c][my_z, 0:1, :] = square
        sum_z[r][c][my_z, 1:2, :] = inner(js[c], snd[2 * r + 1][c])

    def stage_image(r, c):
        drain(rcv[2 * r + 1][c], ex_r.at[2 * r + 1, c])
        square = difference(2 * r + 1, c, ds[c])
        product(shared, shared, into_slots(gs[c]))
        sum_z[r][c][my_z, 2:3, :] = square
        sum_z[r][c][my_z, 3:4, :] = inner(ds[c], gs[c])
        if r == 0 and c == 0:
            hear(1)
            assert len(told) <= 2
        for d in z_order:
            z_copy(r, c, d).start()
        product(joint, shared, into_rows(mine[r][c][2]))
        share(r, c, 2)

    def stage_sums(r, c):
        for i in range(2):
            drain(all_of[r][c][i].at[pl.ds(0, harms - 1)], a_r.at[r, c, i])
        drain(sum_z[r][c].at[pl.ds(0, nz - 1)], z_r.at[r, c])
        sum_y[r][c][my_y * harms + harm] = jnp.sum(sum_z[r][c][...], axis=0)
        for peer in plane_peers:
            y_copy(r, c, peer).start()

    def stage_contact(r, c):
        drain(sum_y[r][c].at[pl.ds(0, NY * harms - 1)], y_r.at[r, c])
        value = sum_y[r][c][0:harms]
        for y in range(1, NY):
            value = value + sum_y[r][c][y * harms : (y + 1) * harms]
        square, curve, square_d, curve_d = (value[:, i : i + 1] for i in range(4))
        first = square / (curve + TINY)
        square = square - 4.0 * first * curve + first * first * square_d
        curve = curve - first * square_d + first * first * curve_d
        second = square / (curve + TINY)
        steps[c][0] = jnp.broadcast_to(first + second, (harms, 8, WIDTH))
        steps[c][1] = jnp.broadcast_to(first * second, (harms, 8, WIDTH))
        drain(all_of[r][c][2].at[pl.ds(0, harms - 1)], a_r.at[r, c, 2])
        contact(r, c)
        for d in h_order:
            from_harm(r, c, d).start()
        bc[r][c][rows_of(harm), :] = oc[r][c][harm]

    def stage_step(r, c):
        both, cross = steps[c][0, harm][0:1], steps[c][1, harm][0:1]

        @pl.loop(0, 2 * MAXB)
        def _(k):
            change = cross * ds[c][k] - both * js[c][k]
            ms[c][k] = change if r == 0 else ms[c][k] + change
            if r + 1 < ROUNDS:
                image = snd[2 * r + 1][c][k]
                tn[c][k] = snd[2 * r][c][k] - both * image + cross * gs[c][k]

        if r + 1 < ROUNDS:
            trace, image, second = (mine[r][c][n][...] for n in range(3))
            mine[r + 1][c][0][...] = trace - both * image + cross * second
        else:

            @pl.loop(0, NB)
            def _(b):
                value = jnp.where(tab[3, b] != 0, ms[c][tab[2, b]], 0.0)
                mo[c][b] = value - jnp.where(tab[5, b] != 0, old[c][tab[4, b]], 0.0)

    def stage_force(r, c):
        drain(bc[r][c].at[pl.ds(0, (harms - 1) * part)], a_r.at[r, c, 3])
        for q in range(CB):
            rows = pl.ds(q * BLK, BLK)
            value = bc[r][c][rows, :] * stc[rows, :]
            old[c][q] = value
            if r + 1 < ROUNDS:
                put(q, value)
            else:
                force[q, :, lanes[c]] = value
        if r + 1 < ROUNDS:
            product(shared, joint, into_slots(snd[2 * r + 2][c], tn[c]))
            send(2 * r + 2, c)
            rows = mine[r + 1][c][0]
            product(joint, joint, into_rows(rows, rows))
            share(r + 1, c, 0)
        else:

            @pl.loop(0, NB)
            def _(b):
                value = jnp.where(tab[5, b] != 0, old[c][tab[4, b]], 0.0)
                mult[b, :, lanes[c]] = mo[c][b] - value

    def settle(r, c):
        if r > 0 or c > 0:
            drain(snd[2 * r][c], ex_s.at[2 * r, c])
        drain(snd[2 * r + 1][c], ex_s.at[2 * r + 1, c])
        drain(sum_y[r][c].at[pl.ds(0, NY * harms - 1)], y_s.at[r, c])
        drain(sum_z[r][c].at[pl.ds(0, nz - 1)], z_s.at[r, c])
        for i in range(3):
            drain(mine[r][c][i].at[pl.ds(0, (harms - 1) * part)], a_s.at[r, c, i])

    def settle_last(r, c):
        drain(oc[r][c].at[pl.ds(0, harms - 1)], a_s.at[r, c, 3])

    for r in range(ROUNDS):
        for c in every:
            stage_jump(r, c)
            if r > 0 and c == NCH - 1:
                for old_c in every:
                    settle(r - 1, old_c)
                    settle_last(r - 1, old_c)
        for c in every:
            stage_image(r, c)
        for c in every:
            stage_sums(r, c)
        for c in every:
            stage_contact(r, c)
            stage_step(r, c)
        if r == ROUNDS - 1:
            for c in every:
                settle(r, c)
        for c in every:
            stage_force(r, c)
    for c in every:
        settle_last(ROUNDS - 1, c)


def per_device(flex, loads, side, partner, contact_blocks, contact_stiff):
    harms = lax.axis_size("harm")
    nz = lax.axis_size("sub") // NY
    part = CROWS // harms
    slots, joint, whole = (
        [pltpu.VMEM((n, BLK, WIDTH), f32)] * NCH for n in (2 * MAXB, CB, NB)
    )
    vmem = lambda *shape: [pltpu.VMEM(shape, f32)] * (NCH * ROUNDS)
    sem = pltpu.SemaphoreType.DMA
    scratch = [
        pltpu.SMEM((1, NB), jnp.int32),
        pltpu.SMEM((1, NB), jnp.int32),
        pltpu.SMEM((1, CB), jnp.int32),
        pltpu.SMEM((6, NB), jnp.int32),
        pltpu.VMEM((1, CROWS), f32),
        pltpu.VMEM((PAIRS, NB, BLK, 128), f32),
        pltpu.VMEM((NB, BLK, COLS), f32),
        pltpu.VMEM((ROWS, ROWS), bf16),
        pltpu.VMEM((ROWS, ROWS), bf16),
        pltpu.VMEM((S_ROWS, 2 * WIDTH), bf16),
        pltpu.VMEM((CROWS, WIDTH), f32),
        pltpu.VMEM((TIMES // 4 + 1, harms, 8, 128), f32),
    ]
    scratch += slots * 5 + [pltpu.VMEM((2, harms, 8, WIDTH), f32)] * NCH + joint + whole
    scratch += slots * (2 * ROUNDS) * 2
    scratch += vmem(nz, 4, WIDTH) + vmem(NY * harms, 4, WIDTH)
    scratch += vmem(harms, part, WIDTH) + vmem(CROWS, WIDTH)
    scratch += vmem(CROWS, WIDTH) * 3 + vmem(harms, part, WIDTH) * 3
    scratch += [sem((6,))]
    scratch += [sem((2 * ROUNDS, NCH))] * 2
    scratch += [sem((ROUNDS, NCH))] * 4
    scratch += [sem((ROUNDS, NCH, 4))] * 2
    scratch += [pltpu.SemaphoreType.REGULAR] * len(relay_steps(nz))
    hbm = pl.BlockSpec(memory_space=pltpu.HBM)
    mult, force = pl.pallas_call(
        functools.partial(kernel, nz, harms),
        out_shape=(
            jax.ShapeDtypeStruct((NB, BLK, COLS), f32),
            jax.ShapeDtypeStruct((CB, BLK, COLS), f32),
        ),
        in_specs=[hbm] * 6,
        out_specs=(OUT, OUT),
        scratch_shapes=scratch,
        compiler_params=pltpu.CompilerParams(
            collective_id=0, has_side_effects=True, vmem_limit_bytes=48 << 20
        ),
    )(
        *(
            pltpu.with_memory_space_constraint(x, pltpu.HBM)
            for x in (
                side,
                partner,
                contact_blocks,
                contact_stiff,
                flex.reshape(NB, BLK, ROWS),
                loads.reshape(NB, BLK, COLS),
            )
        )
    )
    return mult.reshape(loads.shape), force.reshape(1, 1, CROWS, COLS)


def solution(mesh):
    return jax.shard_map(
        per_device,
        mesh=mesh,
        in_specs=(
            P("sub", "harm", None, None),
            P("sub", "harm", None, None),
            P("sub", None),
            P("sub", None),
            P("sub", None),
            P("sub", None),
        ),
        out_specs=(P("sub", "harm", None, None), P("sub", "harm", None, None)),
        check_vma=False,
    )
```

```python
import functools
import math

import jax
import jax.numpy as jnp
from jax import lax
from jax.experimental import pallas as pl
from jax.experimental.pallas import tpu as pltpu
from jax.sharding import PartitionSpec as P

MESH = pl.DeviceIdType.MESH
TIMES = 64
ROUNDS = 2
TINY = 1e-6
NB = 12
BLK = 64
ROWS = NB * BLK
COLS = 256
MAXB = 4
CB = 4
CROWS = CB * BLK
NY = 4
NCH = 2
WIDTH = COLS // NCH
S_ROWS = 2 * MAXB * BLK
TILE = 128
PAIRS = ROWS // 128
OUT = pl.BlockSpec(memory_space=pltpu.VMEM)

f32 = jnp.float32
bf16 = jnp.bfloat16


def dot(a, b):
    return jnp.dot(a, b, preferred_element_type=f32)


def split(x):
    high = x.astype(bf16)
    return high, (x - high.astype(f32)).astype(bf16)


def cube_law(coefs, table, odd_lane):
    harms = len(coefs)
    out = [None] * harms

    def plus(x, y):
        return y if x is None else x + y

    def cubes(y):
        square = y * y
        turned = pltpu.roll(square, 127, axis=2), pltpu.roll(square, 1, axis=2)
        return y * (square + 3.0 * jnp.where(odd_lane, turned[1], turned[0]))

    for t in range(TIMES // 4 + 1):
        parity = [None, None]
        for k in range(harms):
            parity[(k + 1) % 2] = plus(parity[(k + 1) % 2], coefs[k] * table[t, k])
        first, second = cubes(parity[0] + parity[1]), cubes(parity[0] - parity[1])
        both = [first + second, first - second]
        if t in (0, TIMES // 4):
            both = [0.5 * x for x in both]
        for k in range(harms):
            out[k] = plus(out[k], both[(k + 1) % 2] * table[t, k])
    return [(4.0 / TIMES) * x for x in out]


def relay_steps(nz):
    radius, steps = min(2, nz // 2), []
    while radius < nz // 2:
        steps.append(radius)
        radius *= 2
    return steps


def drain(ref, sem):
    pltpu.make_async_copy(ref, ref, sem).wait()


def signal(sem, peer):
    pl.semaphore_signal(sem, inc=1, device_id=peer, device_id_type=MESH)


def kernel(nz, harms, side_h, partner_h, cblk_h, stiff_h, flex_h, loads_h, mult, force, *scratch):
    names = iter(scratch)
    take = lambda n: [next(names) for _ in range(n)]
    side, partner, cblk, tab = take(4)
    stiff, flex, loads, fh, fl, x2, stc, waves = take(8)
    js, ds, gs, tn, ms = (take(NCH) for _ in range(5))
    steps, old, mo = (take(NCH) for _ in range(3))
    snd = [take(NCH) for _ in range(2 * ROUNDS)]
    rcv = [take(NCH) for _ in range(2 * ROUNDS)]
    sum_z, sum_y, oc, bc = ([take(NCH) for _ in range(ROUNDS)] for _ in range(4))
    mine = [[take(3) for _ in range(NCH)] for _ in range(ROUNDS)]
    all_of = [[take(3) for _ in range(NCH)] for _ in range(ROUNDS)]
    in_sem, ex_s, ex_r, y_s, y_r, z_s, z_r, a_s, a_r = take(9)
    told = take(len(relay_steps(nz)))

    part = CROWS // harms
    sub = lax.axis_index("sub")
    harm = lax.axis_index("harm")
    subs = nz * NY
    my_y = lax.rem(sub, NY)
    my_z = sub // NY
    right = (lax.rem(sub + 1, subs), harm)
    left = (lax.rem(sub + subs - 1, subs), harm)
    y_peers = [(my_z * NY + lax.rem(my_y + d, NY), harm) for d in range(1, NY)]
    pairs = [(d, h) for d in range(NY) for h in range(harms) if d + h > 0]
    pairs.sort(key=lambda p: -min(p[0], NY - p[0]) - min(p[1], harms - p[1]) / 2)
    plane_peers = [
        (my_z * NY + lax.rem(my_y + d, NY), lax.rem(harm + h, harms)) for d, h in pairs
    ]
    z_order = sorted(range(1, nz), key=lambda d: -min(d, nz - d))
    z_peers = {d: (lax.rem(my_z + d, nz) * NY + my_y, harm) for d in z_order}
    h_order = sorted(range(1, harms), key=lambda d: -min(d, harms - d))
    h_peers = {d: lax.rem(harm + d, harms) for d in h_order}

    copies = [
        pltpu.make_async_copy(one, two, in_sem.at[i])
        for i, (one, two) in enumerate(
            (
                (side_h, side),
                (partner_h, partner),
                (cblk_h, cblk),
                (loads_h, loads),
                (stiff_h, stiff),
            )
        )
    ]
    copies += [
        pltpu.make_async_copy(
            flex_h.at[:, :, pl.ds(128 * i, 128)], flex.at[i], in_sem.at[len(copies)]
        )
        for i in range(PAIRS)
    ]
    barrier = pltpu.get_barrier_semaphore()
    near = [d for d in z_order if min(d, nz - d) <= 2]
    greet = [right, left] + [z_peers[d] for d in near] + y_peers + [(sub, h_peers[d]) for d in h_order]
    for peer in greet:
        signal(barrier, peer)

    for copy in copies:
        copy.start()
    for copy in copies[:3]:
        copy.wait()

    sides = [side[0, b] for b in range(NB)]
    partners = [partner[0, b] for b in range(NB)]
    contacts = [cblk[0, q] for q in range(CB)]
    one, zero = jnp.int32(1), jnp.int32(0)
    ranks = []
    count_r = count_l = zero
    for b in range(NB):
        rank = zero
        for other in range(NB):
            if other != b:
                before = (sides[other] == -1) & (partners[other] < partners[b])
                rank = rank + jnp.where(before, one, zero)
        is_r, is_l = sides[b] == 1, sides[b] == -1
        slot = jnp.where(is_r, count_r, jnp.where(is_l, MAXB + rank, zero))
        slot = jnp.minimum(slot, 2 * MAXB - 1)
        count_r = count_r + jnp.where(is_r, one, zero)
        count_l = count_l + jnp.where(is_l, one, zero)
        ranks.append(jnp.where(sides[b] != 0, slot, -1))
        tab[2, b] = slot
        tab[3, b] = jnp.where(sides[b] != 0, one, zero)
    for k in range(2 * MAXB):
        block = zero
        for b in range(NB):
            block = jnp.where(ranks[b] == k, b, block)
        tab[0, k] = block
        tab[1, k] = jnp.where(k % MAXB < (count_r if k < MAXB else count_l), one, zero)
    for q in range(CB):
        tab[0, 2 * MAXB + q] = contacts[q]
    def exchange(e, c, way):
        return pltpu.make_async_remote_copy(
            src_ref=snd[e][c].at[pl.ds(way * MAXB, MAXB)],
            dst_ref=rcv[e][c].at[pl.ds((1 - way) * MAXB, MAXB)],
            send_sem=ex_s.at[e, c],
            recv_sem=ex_r.at[e, c],
            device_id=right if way == 0 else left,
            device_id_type=MESH,
        )

    def tell(i):
        steps = relay_steps(nz)
        if i < len(steps):
            signal(told[i], z_peers[steps[i]])
            signal(told[i], z_peers[nz - steps[i]])

    def hear(i):
        if i < len(told):
            pl.semaphore_wait(told[i], 2)
            tell(i + 1)

    def send(e, c):
        for way in range(2):
            exchange(e, c, way).start()

    copies[3].wait()
    lanes = [pl.ds(c * WIDTH, WIDTH) for c in range(NCH)]

    for c in range(NCH):

        @pl.loop(0, 2 * MAXB)
        def _(k):
            snd[0][c][k] = loads[tab[0, k], :, lanes[c]]

    pl.semaphore_wait(barrier, len(greet))
    send(0, 0)
    tell(0)

    for b in range(NB):
        place = found = zero
        for q in range(CB):
            same = contacts[q] == b
            place = jnp.where(same, q, place)
            found = jnp.where(same, one, found)
        tab[4, b] = place
        tab[5, b] = found

    def rows_of(index):
        return pl.ds(pl.multiple_of(index * part, part), part)

    def to_harm(r, c, i, d):
        return pltpu.make_async_remote_copy(
            src_ref=mine[r][c][i].at[rows_of(h_peers[d])],
            dst_ref=all_of[r][c][i].at[harm],
            send_sem=a_s.at[r, c, i],
            recv_sem=a_r.at[r, c, i],
            device_id=(sub, h_peers[d]),
            device_id_type=MESH,
        )

    def share(r, c, i):
        for d in h_order:
            to_harm(r, c, i, d).start()
        all_of[r][c][i][harm] = mine[r][c][i][rows_of(harm), :]

    for c in range(NCH):
        for q in range(CB):
            mine[0][c][0][pl.ds(q * BLK, BLK), :] = loads[cblk[0, q], :, lanes[c]]
        share(0, c, 0)

    drain(flex, in_sem.at[5])
    lane = lax.broadcasted_iota(jnp.int32, (BLK, 128), 1)

    @pl.loop(0, 2 * MAXB + CB)
    def _(k):
        place = pl.ds(pl.multiple_of(k * BLK, BLK), BLK)

        def half(block, odd):
            pair = lax.div(block, jnp.int32(2))
            value = flex[pair, tab[0, k]]
            turned = pltpu.roll(value, 64, axis=1)
            return jnp.where(block - 2 * pair == odd, value, turned)

        for i in range(PAIRS):
            value = jnp.where(lane < 64, half(tab[0, 2 * i], 0), half(tab[0, 2 * i + 1], 1))
            cols = slice(128 * i, 128 * i + 128)
            fh[place, cols], fl[place, cols] = split(value)

    hear(0)
    drain(snd[0][0], ex_s.at[0, 0])
    send(0, 1)

    odd_lane = lax.broadcasted_iota(jnp.int32, (8, 128), 1) % 2 == 1
    for t in range(TIMES // 4 + 1):
        for k in range(harms):
            angle = 2 * math.pi * t * (k + 1) / TIMES
            waves[t, k] = jnp.where(odd_lane, math.sin(angle), math.cos(angle)).astype(f32)
    copies[4].wait()
    row = lax.broadcasted_iota(jnp.int32, (CROWS, CROWS), 0)
    col = lax.broadcasted_iota(jnp.int32, (CROWS, CROWS), 1)
    column = jnp.sum(jnp.where(row == col, stiff[...], 0.0), axis=1, keepdims=True)
    stc[...] = jnp.broadcast_to(column, (CROWS, WIDTH))

    def fold(x):
        return jnp.sum(x.reshape(BLK // 8, 8, WIDTH), axis=0)

    def put(k, value):
        rows = pl.ds(pl.multiple_of(k * BLK, BLK), BLK)
        x2[rows, :WIDTH], x2[rows, WIDTH:] = split(value)

    def total(acc):
        return jnp.sum(acc, axis=0, keepdims=True)

    def difference(e, c, target):
        def step(k, acc):
            value = snd[e][c][k] - rcv[e][c][k]
            value = jnp.where(tab[1, k] != 0, value, 0.0)
            target[k] = value
            put(k, value)
            return acc + fold(value * value)

        return total(lax.fori_loop(0, 2 * MAXB, step, jnp.zeros((8, WIDTH), f32)))

    def inner(one, two):
        acc = jnp.zeros((8, WIDTH), f32)
        return total(lax.fori_loop(0, 2 * MAXB, lambda k, a: a + fold(one[k] * two[k]), acc))

    def product(rows, cols, put_tile):
        x = x2[0 : cols[1] - cols[0], :]
        for at in range(rows[0], rows[1], TILE):
            first = fh[at : at + TILE, cols[0] : cols[1]]
            second = fl[at : at + TILE, cols[0] : cols[1]]
            out = dot(first, x) + dot(second, x)
            put_tile(at - rows[0], out[:, :WIDTH] + out[:, WIDTH:])

    def into_slots(target, base=None):
        def put_tile(at, out):
            blocks = pl.ds(at // BLK, TILE // BLK)
            out = out.reshape(TILE // BLK, BLK, WIDTH)
            target[blocks] = out if base is None else base[blocks] - out

        return put_tile

    def into_rows(target, base=None):
        def put_tile(at, out):
            rows = pl.ds(at, TILE)
            target[rows, :] = out if base is None else base[rows, :] - out

        return put_tile

    def y_copy(r, c, peer):
        ref = sum_y[r][c].at[my_y * harms + harm]
        return pltpu.make_async_remote_copy(
            src_ref=ref,
            dst_ref=ref,
            send_sem=y_s.at[r, c],
            recv_sem=y_r.at[r, c],
            device_id=peer,
            device_id_type=MESH,
        )

    def z_copy(r, c, d):
        ref = sum_z[r][c].at[my_z]
        return pltpu.make_async_remote_copy(
            src_ref=ref,
            dst_ref=ref,
            send_sem=z_s.at[r, c],
            recv_sem=z_r.at[r, c],
            device_id=z_peers[d],
            device_id_type=MESH,
        )

    def from_harm(r, c, d):
        return pltpu.make_async_remote_copy(
            src_ref=oc[r][c].at[h_peers[d]],
            dst_ref=bc[r][c].at[rows_of(harm)],
            send_sem=a_s.at[r, c, 3],
            recv_sem=a_r.at[r, c, 3],
            device_id=(sub, h_peers[d]),
            device_id_type=MESH,
        )

    def contact(r, c):
        odd = jnp.broadcast_to(odd_lane, (2, 8, 128))

        @pl.loop(0, part // 16)
        def _(i):
            rows = pl.ds(pl.multiple_of(i * 16, 16), 16)
            coefs = []
            for k in range(harms):
                trace, image, second = (
                    all_of[r][c][n][k, rows, :].reshape(2, 8, 128) for n in range(3)
                )
                coefs.append(trace - steps[c][0, k] * image + steps[c][1, k] * second)
            for k, value in enumerate(cube_law(coefs, waves, odd)):
                oc[r][c][k, rows, :] = value.reshape(16, 128)

    shared, joint, every = (0, S_ROWS), (S_ROWS, ROWS), range(NCH)

    def stage_jump(r, c):
        drain(rcv[2 * r][c], ex_r.at[2 * r, c])
        square = difference(2 * r, c, js[c])
        product(shared, shared, into_slots(snd[2 * r + 1][c]))
        send(2 * r + 1, c)
        product(joint, shared, into_rows(mine[r][c][1]))
        share(r, c, 1)
        sum_z[r][c][my_z, 0:1, :] = square
        sum_z[r][c][my_z, 1:2, :] = inner(js[c], snd[2 * r + 1][c])

    def stage_image(r, c):
        drain(rcv[2 * r + 1][c], ex_r.at[2 * r + 1, c])
        square = difference(2 * r + 1, c, ds[c])
        product(shared, shared, into_slots(gs[c]))
        sum_z[r][c][my_z, 2:3, :] = square
        sum_z[r][c][my_z, 3:4, :] = inner(ds[c], gs[c])
        if r == 0 and c == 0:
            hear(1)
            assert len(told) <= 2
        for d in z_order:
            z_copy(r, c, d).start()
        product(joint, shared, into_rows(mine[r][c][2]))
        share(r, c, 2)

    def stage_sums(r, c):
        for i in range(2):
            drain(all_of[r][c][i].at[pl.ds(0, harms - 1)], a_r.at[r, c, i])
        drain(sum_z[r][c].at[pl.ds(0, nz - 1)], z_r.at[r, c])
        sum_y[r][c][my_y * harms + harm] = jnp.sum(sum_z[r][c][...], axis=0)
        for peer in plane_peers:
            y_copy(r, c, peer).start()

    def stage_contact(r, c):
        drain(sum_y[r][c].at[pl.ds(0, NY * harms - 1)], y_r.at[r, c])
        value = sum_y[r][c][0:harms]
        for y in range(1, NY):
            value = value + sum_y[r][c][y * harms : (y + 1) * harms]
        square, curve, square_d, curve_d = (value[:, i : i + 1] for i in range(4))
        first = square / (curve + TINY)
        square = square - 4.0 * first * curve + first * first * square_d
        curve = curve - first * square_d + first * first * curve_d
        second = square / (curve + TINY)
        steps[c][0] = jnp.broadcast_to(first + second, (harms, 8, WIDTH))
        steps[c][1] = jnp.broadcast_to(first * second, (harms, 8, WIDTH))
        drain(all_of[r][c][2].at[pl.ds(0, harms - 1)], a_r.at[r, c, 2])
        contact(r, c)
        for d in h_order:
            from_harm(r, c, d).start()
        bc[r][c][rows_of(harm), :] = oc[r][c][harm]

    def stage_step(r, c):
        both, cross = steps[c][0, harm][0:1], steps[c][1, harm][0:1]

        @pl.loop(0, 2 * MAXB)
        def _(k):
            change = cross * ds[c][k] - both * js[c][k]
            ms[c][k] = change if r == 0 else ms[c][k] + change
            if r + 1 < ROUNDS:
                image = snd[2 * r + 1][c][k]
                tn[c][k] = snd[2 * r][c][k] - both * image + cross * gs[c][k]

        if r + 1 < ROUNDS:
            trace, image, second = (mine[r][c][n][...] for n in range(3))
            mine[r + 1][c][0][...] = trace - both * image + cross * second
        else:

            @pl.loop(0, NB)
            def _(b):
                value = jnp.where(tab[3, b] != 0, ms[c][tab[2, b]], 0.0)
                mo[c][b] = value - jnp.where(tab[5, b] != 0, old[c][tab[4, b]], 0.0)

    def stage_force(r, c):
        drain(bc[r][c].at[pl.ds(0, (harms - 1) * part)], a_r.at[r, c, 3])
        for q in range(CB):
            rows = pl.ds(q * BLK, BLK)
            value = bc[r][c][rows, :] * stc[rows, :]
            old[c][q] = value
            if r + 1 < ROUNDS:
                put(q, value)
            else:
                force[q, :, lanes[c]] = value
        if r + 1 < ROUNDS:
            product(shared, joint, into_slots(snd[2 * r + 2][c], tn[c]))
            send(2 * r + 2, c)
            rows = mine[r + 1][c][0]
            product(joint, joint, into_rows(rows, rows))
            share(r + 1, c, 0)
        else:

            @pl.loop(0, NB)
            def _(b):
                value = jnp.where(tab[5, b] != 0, old[c][tab[4, b]], 0.0)
                mult[b, :, lanes[c]] = mo[c][b] - value

    def settle(r, c):
        if r > 0 or c > 0:
            drain(snd[2 * r][c], ex_s.at[2 * r, c])
        drain(snd[2 * r + 1][c], ex_s.at[2 * r + 1, c])
        drain(sum_y[r][c].at[pl.ds(0, NY * harms - 1)], y_s.at[r, c])
        drain(sum_z[r][c].at[pl.ds(0, nz - 1)], z_s.at[r, c])
        for i in range(3):
            drain(mine[r][c][i].at[pl.ds(0, (harms - 1) * part)], a_s.at[r, c, i])

    def settle_last(r, c):
        drain(oc[r][c].at[pl.ds(0, harms - 1)], a_s.at[r, c, 3])

    for r in range(ROUNDS):
        for c in every:
            stage_jump(r, c)
            if r > 0 and c == NCH - 1:
                for old_c in every:
                    settle(r - 1, old_c)
                    settle_last(r - 1, old_c)
        for c in every:
            stage_image(r, c)
        for c in every:
            stage_sums(r, c)
        for c in every:
            stage_contact(r, c)
            stage_step(r, c)
        if r == ROUNDS - 1:
            for c in every:
                settle(r, c)
        for c in every:
            stage_force(r, c)
    for c in every:
        settle_last(ROUNDS - 1, c)


def write_out(mult_v, force_v, mult, force, sem):
    copies = [
        pltpu.make_async_copy(mult_v, mult, sem.at[0]),
        pltpu.make_async_copy(force_v, force, sem.at[1]),
    ]
    for copy in copies:
        copy.start()
    for copy in copies:
        copy.wait()


def per_device(flex, loads, side, partner, contact_blocks, contact_stiff):
    harms = lax.axis_size("harm")
    nz = lax.axis_size("sub") // NY
    part = CROWS // harms
    slots, joint, whole = (
        [pltpu.VMEM((n, BLK, WIDTH), f32)] * NCH for n in (2 * MAXB, CB, NB)
    )
    vmem = lambda *shape: [pltpu.VMEM(shape, f32)] * (NCH * ROUNDS)
    sem = pltpu.SemaphoreType.DMA
    scratch = [
        pltpu.SMEM((1, NB), jnp.int32),
        pltpu.SMEM((1, NB), jnp.int32),
        pltpu.SMEM((1, CB), jnp.int32),
        pltpu.SMEM((6, NB), jnp.int32),
        pltpu.VMEM((1, CROWS), f32),
        pltpu.VMEM((PAIRS, NB, BLK, 128), f32),
        pltpu.VMEM((NB, BLK, COLS), f32),
        pltpu.VMEM((ROWS, ROWS), bf16),
        pltpu.VMEM((ROWS, ROWS), bf16),
        pltpu.VMEM((S_ROWS, 2 * WIDTH), bf16),
        pltpu.VMEM((CROWS, WIDTH), f32),
        pltpu.VMEM((TIMES // 4 + 1, harms, 8, 128), f32),
    ]
    scratch += slots * 5 + [pltpu.VMEM((2, harms, 8, WIDTH), f32)] * NCH + joint + whole
    scratch += slots * (2 * ROUNDS) * 2
    scratch += vmem(nz, 4, WIDTH) + vmem(NY * harms, 4, WIDTH)
    scratch += vmem(harms, part, WIDTH) + vmem(CROWS, WIDTH)
    scratch += vmem(CROWS, WIDTH) * 3 + vmem(harms, part, WIDTH) * 3
    scratch += [sem((6,))]
    scratch += [sem((2 * ROUNDS, NCH))] * 2
    scratch += [sem((ROUNDS, NCH))] * 4
    scratch += [sem((ROUNDS, NCH, 4))] * 2
    scratch += [pltpu.SemaphoreType.REGULAR] * len(relay_steps(nz))
    hbm = pl.BlockSpec(memory_space=pltpu.HBM)
    mult, force = pl.pallas_call(
        functools.partial(kernel, nz, harms),
        out_shape=(
            jax.ShapeDtypeStruct((NB, BLK, COLS), f32),
            jax.ShapeDtypeStruct((CB, BLK, COLS), f32),
        ),
        in_specs=[hbm] * 6,
        out_specs=(OUT, OUT),
        scratch_shapes=scratch,
        compiler_params=pltpu.CompilerParams(
            collective_id=0, has_side_effects=True, vmem_limit_bytes=48 << 20
        ),
    )(
        *(
            pltpu.with_memory_space_constraint(x, pltpu.HBM)
            for x in (
                side,
                partner,
                contact_blocks,
                contact_stiff,
                flex.reshape(NB, BLK, ROWS),
                loads.reshape(NB, BLK, COLS),
            )
        )
    )
    mult, force = pl.pallas_call(
        write_out,
        out_shape=(
            jax.ShapeDtypeStruct((NB, BLK, COLS), f32),
            jax.ShapeDtypeStruct((CB, BLK, COLS), f32),
        ),
        in_specs=[pl.BlockSpec(memory_space=pl.ANY)] * 2,
        out_specs=[pl.BlockSpec(memory_space=pl.ANY)] * 2,
        scratch_shapes=[pltpu.SemaphoreType.DMA((2,))],
        compiler_params=pltpu.CompilerParams(vmem_limit_bytes=1 << 20),
    )(mult, force)
    return mult.reshape(loads.shape), force.reshape(1, 1, CROWS, COLS)


def solution(mesh):
    return jax.shard_map(
        per_device,
        mesh=mesh,
        in_specs=(
            P("sub", "harm", None, None),
            P("sub", "harm", None, None),
            P("sub", None),
            P("sub", None),
            P("sub", None),
            P("sub", None),
        ),
        out_specs=(P("sub", "harm", None, None), P("sub", "harm", None, None)),
        check_vma=False,
    )
```

```python
import functools
import math

import jax
import jax.numpy as jnp
from jax import lax
from jax.experimental import pallas as pl
from jax.experimental.pallas import tpu as pltpu
from jax.sharding import PartitionSpec as P

MESH = pl.DeviceIdType.MESH
TIMES = 64
ROUNDS = 2
TINY = 1e-6
NB = 12
BLK = 64
ROWS = NB * BLK
COLS = 256
MAXB = 4
CB = 4
CROWS = CB * BLK
NY = 4
NCH = 2
WIDTH = COLS // NCH
S_ROWS = 2 * MAXB * BLK
TILE = 128
PAIRS = ROWS // 128
OUT = pl.BlockSpec(memory_space=pltpu.VMEM)

f32 = jnp.float32
bf16 = jnp.bfloat16


def dot(a, b):
    return jnp.dot(a, b, preferred_element_type=f32)


def split(x):
    high = x.astype(bf16)
    return high, (x - high.astype(f32)).astype(bf16)


def cube_law(coefs, table, odd_lane):
    harms = len(coefs)
    out = [None] * harms

    def plus(x, y):
        return y if x is None else x + y

    def cubes(y):
        square = y * y
        turned = pltpu.roll(square, 127, axis=2), pltpu.roll(square, 1, axis=2)
        return y * (square + 3.0 * jnp.where(odd_lane, turned[1], turned[0]))

    for t in range(TIMES // 4 + 1):
        parity = [None, None]
        for k in range(harms):
            parity[(k + 1) % 2] = plus(parity[(k + 1) % 2], coefs[k] * table[t, k])
        first, second = cubes(parity[0] + parity[1]), cubes(parity[0] - parity[1])
        both = [first + second, first - second]
        if t in (0, TIMES // 4):
            both = [0.5 * x for x in both]
        for k in range(harms):
            out[k] = plus(out[k], both[(k + 1) % 2] * table[t, k])
    return [(4.0 / TIMES) * x for x in out]


def relay_steps(nz):
    radius, steps = min(2, nz // 2), []
    while radius < nz // 2:
        steps.append(radius)
        radius *= 2
    return steps


def drain(ref, sem):
    pltpu.make_async_copy(ref, ref, sem).wait()


def signal(sem, peer):
    pl.semaphore_signal(sem, inc=1, device_id=peer, device_id_type=MESH)


def kernel(nz, harms, side_h, partner_h, cblk_h, stiff_h, flex_h, loads_h, mult, force, *scratch):
    names = iter(scratch)
    take = lambda n: [next(names) for _ in range(n)]
    side, partner, cblk, tab = take(4)
    stiff, flex, loads, fh, fl, x2, stc, waves = take(8)
    js, ds, gs, tn, ms = (take(NCH) for _ in range(5))
    steps, old, mo = (take(NCH) for _ in range(3))
    snd = [take(NCH) for _ in range(2 * ROUNDS)]
    rcv = [take(NCH) for _ in range(2 * ROUNDS)]
    sum_z, sum_y, oc, bc = ([take(NCH) for _ in range(ROUNDS)] for _ in range(4))
    mine = [[take(3) for _ in range(NCH)] for _ in range(ROUNDS)]
    all_of = [[take(3) for _ in range(NCH)] for _ in range(ROUNDS)]
    in_sem, ex_s, ex_r, y_s, y_r, z_s, z_r, a_s, a_r = take(9)
    told = take(len(relay_steps(nz)))

    part = CROWS // harms
    sub = lax.axis_index("sub")
    harm = lax.axis_index("harm")
    subs = nz * NY
    my_y = lax.rem(sub, NY)
    my_z = sub // NY
    right = (lax.rem(sub + 1, subs), harm)
    left = (lax.rem(sub + subs - 1, subs), harm)
    y_peers = [(my_z * NY + lax.rem(my_y + d, NY), harm) for d in range(1, NY)]
    pairs = [(d, h) for d in range(NY) for h in range(harms) if d + h > 0]
    pairs.sort(key=lambda p: -min(p[0], NY - p[0]) - min(p[1], harms - p[1]) / 2)
    plane_peers = [
        (my_z * NY + lax.rem(my_y + d, NY), lax.rem(harm + h, harms)) for d, h in pairs
    ]
    z_order = sorted(range(1, nz), key=lambda d: -min(d, nz - d))
    z_peers = {d: (lax.rem(my_z + d, nz) * NY + my_y, harm) for d in z_order}
    h_order = sorted(range(1, harms), key=lambda d: -min(d, harms - d))
    h_peers = {d: lax.rem(harm + d, harms) for d in h_order}

    copies = [
        pltpu.make_async_copy(one, two, in_sem.at[i])
        for i, (one, two) in enumerate(
            (
                (side_h, side),
                (partner_h, partner),
                (cblk_h, cblk),
                (loads_h, loads),
                (stiff_h, stiff),
            )
        )
    ]
    copies += [
        pltpu.make_async_copy(
            flex_h.at[:, :, pl.ds(128 * i, 128)], flex.at[i], in_sem.at[len(copies)]
        )
        for i in range(PAIRS)
    ]
    barrier = pltpu.get_barrier_semaphore()
    near = [d for d in z_order if min(d, nz - d) <= 2]
    greet = [right, left] + [z_peers[d] for d in near] + y_peers + [(sub, h_peers[d]) for d in h_order]
    for peer in greet:
        signal(barrier, peer)

    for copy in copies:
        copy.start()
    for copy in copies[:3]:
        copy.wait()

    sides = [side[0, b] for b in range(NB)]
    partners = [partner[0, b] for b in range(NB)]
    contacts = [cblk[0, q] for q in range(CB)]
    one, zero = jnp.int32(1), jnp.int32(0)
    ranks = []
    count_r = count_l = zero
    for b in range(NB):
        rank = zero
        for other in range(NB):
            if other != b:
                before = (sides[other] == -1) & (partners[other] < partners[b])
                rank = rank + jnp.where(before, one, zero)
        is_r, is_l = sides[b] == 1, sides[b] == -1
        slot = jnp.where(is_r, count_r, jnp.where(is_l, MAXB + rank, zero))
        slot = jnp.minimum(slot, 2 * MAXB - 1)
        count_r = count_r + jnp.where(is_r, one, zero)
        count_l = count_l + jnp.where(is_l, one, zero)
        ranks.append(jnp.where(sides[b] != 0, slot, -1))
        tab[2, b] = slot
        tab[3, b] = jnp.where(sides[b] != 0, one, zero)
    for k in range(2 * MAXB):
        block = zero
        for b in range(NB):
            block = jnp.where(ranks[b] == k, b, block)
        tab[0, k] = block
        tab[1, k] = jnp.where(k % MAXB < (count_r if k < MAXB else count_l), one, zero)
    for q in range(CB):
        tab[0, 2 * MAXB + q] = contacts[q]
    def exchange(e, c, way, half):
        return pltpu.make_async_remote_copy(
            src_ref=snd[e][c].at[pl.ds(way * MAXB + 2 * half, 2)],
            dst_ref=rcv[e][c].at[pl.ds((1 - way) * MAXB + 2 * half, 2)],
            send_sem=ex_s.at[e, c],
            recv_sem=ex_r.at[e, c],
            device_id=right if way == 0 else left,
            device_id_type=MESH,
        )

    def tell(i):
        steps = relay_steps(nz)
        if i < len(steps):
            signal(told[i], z_peers[steps[i]])
            signal(told[i], z_peers[nz - steps[i]])

    def hear(i):
        if i < len(told):
            pl.semaphore_wait(told[i], 2)
            tell(i + 1)

    def send(e, c):
        for half in range(2):
            for way in range(2):
                exchange(e, c, way, half).start()

    copies[3].wait()
    lanes = [pl.ds(c * WIDTH, WIDTH) for c in range(NCH)]

    for c in range(NCH):

        @pl.loop(0, 2 * MAXB)
        def _(k):
            snd[0][c][k] = loads[tab[0, k], :, lanes[c]]

    pl.semaphore_wait(barrier, len(greet))
    send(0, 0)
    tell(0)

    for b in range(NB):
        place = found = zero
        for q in range(CB):
            same = contacts[q] == b
            place = jnp.where(same, q, place)
            found = jnp.where(same, one, found)
        tab[4, b] = place
        tab[5, b] = found

    def rows_of(index):
        return pl.ds(pl.multiple_of(index * part, part), part)

    def to_harm(r, c, i, d):
        return pltpu.make_async_remote_copy(
            src_ref=mine[r][c][i].at[rows_of(h_peers[d])],
            dst_ref=all_of[r][c][i].at[harm],
            send_sem=a_s.at[r, c, i],
            recv_sem=a_r.at[r, c, i],
            device_id=(sub, h_peers[d]),
            device_id_type=MESH,
        )

    def share(r, c, i):
        for d in h_order:
            to_harm(r, c, i, d).start()
        all_of[r][c][i][harm] = mine[r][c][i][rows_of(harm), :]

    for c in range(NCH):
        for q in range(CB):
            mine[0][c][0][pl.ds(q * BLK, BLK), :] = loads[cblk[0, q], :, lanes[c]]
        share(0, c, 0)

    drain(flex, in_sem.at[5])
    lane = lax.broadcasted_iota(jnp.int32, (BLK, 128), 1)

    @pl.loop(0, 2 * MAXB + CB)
    def _(k):
        place = pl.ds(pl.multiple_of(k * BLK, BLK), BLK)

        def half(block, odd):
            pair = lax.div(block, jnp.int32(2))
            value = flex[pair, tab[0, k]]
            turned = pltpu.roll(value, 64, axis=1)
            return jnp.where(block - 2 * pair == odd, value, turned)

        for i in range(PAIRS):
            value = jnp.where(lane < 64, half(tab[0, 2 * i], 0), half(tab[0, 2 * i + 1], 1))
            cols = slice(128 * i, 128 * i + 128)
            fh[place, cols], fl[place, cols] = split(value)

    hear(0)
    drain(snd[0][0], ex_s.at[0, 0])
    send(0, 1)

    odd_lane = lax.broadcasted_iota(jnp.int32, (8, 128), 1) % 2 == 1
    for t in range(TIMES // 4 + 1):
        for k in range(harms):
            angle = 2 * math.pi * t * (k + 1) / TIMES
            waves[t, k] = jnp.where(odd_lane, math.sin(angle), math.cos(angle)).astype(f32)
    copies[4].wait()
    row = lax.broadcasted_iota(jnp.int32, (CROWS, CROWS), 0)
    col = lax.broadcasted_iota(jnp.int32, (CROWS, CROWS), 1)
    column = jnp.sum(jnp.where(row == col, stiff[...], 0.0), axis=1, keepdims=True)
    stc[...] = jnp.broadcast_to(column, (CROWS, WIDTH))

    def fold(x):
        return jnp.sum(x.reshape(BLK // 8, 8, WIDTH), axis=0)

    def put(k, value):
        rows = pl.ds(pl.multiple_of(k * BLK, BLK), BLK)
        x2[rows, :WIDTH], x2[rows, WIDTH:] = split(value)

    def total(acc):
        return jnp.sum(acc, axis=0, keepdims=True)

    def difference(e, c, target):
        def step(k, acc):
            value = snd[e][c][k] - rcv[e][c][k]
            value = jnp.where(tab[1, k] != 0, value, 0.0)
            target[k] = value
            put(k, value)
            return acc + fold(value * value)

        return total(lax.fori_loop(0, 2 * MAXB, step, jnp.zeros((8, WIDTH), f32)))

    def inner(one, two):
        acc = jnp.zeros((8, WIDTH), f32)
        return total(lax.fori_loop(0, 2 * MAXB, lambda k, a: a + fold(one[k] * two[k]), acc))

    def product(rows, cols, put_tile):
        x = x2[0 : cols[1] - cols[0], :]
        tiles = list(range(rows[0], rows[1], TILE))
        for at in tiles[0::2] + tiles[1::2]:
            first = fh[at : at + TILE, cols[0] : cols[1]]
            second = fl[at : at + TILE, cols[0] : cols[1]]
            out = dot(first, x) + dot(second, x)
            put_tile(at - rows[0], out[:, :WIDTH] + out[:, WIDTH:])

    def into_slots(target, base=None, sent=None):
        def put_tile(at, out):
            blocks = pl.ds(at // BLK, TILE // BLK)
            out = out.reshape(TILE // BLK, BLK, WIDTH)
            target[blocks] = out if base is None else base[blocks] - out
            if sent is not None:
                first = at // BLK
                exchange(*sent, first // MAXB, first % MAXB // 2).start()

        return put_tile

    def into_rows(target, base=None):
        def put_tile(at, out):
            rows = pl.ds(at, TILE)
            target[rows, :] = out if base is None else base[rows, :] - out

        return put_tile

    def y_copy(r, c, peer):
        ref = sum_y[r][c].at[my_y * harms + harm]
        return pltpu.make_async_remote_copy(
            src_ref=ref,
            dst_ref=ref,
            send_sem=y_s.at[r, c],
            recv_sem=y_r.at[r, c],
            device_id=peer,
            device_id_type=MESH,
        )

    def z_copy(r, c, d):
        ref = sum_z[r][c].at[my_z]
        return pltpu.make_async_remote_copy(
            src_ref=ref,
            dst_ref=ref,
            send_sem=z_s.at[r, c],
            recv_sem=z_r.at[r, c],
            device_id=z_peers[d],
            device_id_type=MESH,
        )

    def from_harm(r, c, d):
        return pltpu.make_async_remote_copy(
            src_ref=oc[r][c].at[h_peers[d]],
            dst_ref=bc[r][c].at[rows_of(harm)],
            send_sem=a_s.at[r, c, 3],
            recv_sem=a_r.at[r, c, 3],
            device_id=(sub, h_peers[d]),
            device_id_type=MESH,
        )

    def contact(r, c):
        odd = jnp.broadcast_to(odd_lane, (2, 8, 128))

        @pl.loop(0, part // 16)
        def _(i):
            rows = pl.ds(pl.multiple_of(i * 16, 16), 16)
            coefs = []
            for k in range(harms):
                trace, image, second = (
                    all_of[r][c][n][k, rows, :].reshape(2, 8, 128) for n in range(3)
                )
                coefs.append(trace - steps[c][0, k] * image + steps[c][1, k] * second)
            for k, value in enumerate(cube_law(coefs, waves, odd)):
                oc[r][c][k, rows, :] = value.reshape(16, 128)

    shared, joint, every = (0, S_ROWS), (S_ROWS, ROWS), range(NCH)

    def stage_jump(r, c):
        drain(rcv[2 * r][c], ex_r.at[2 * r, c])
        square = difference(2 * r, c, js[c])
        product(shared, shared, into_slots(snd[2 * r + 1][c], sent=(2 * r + 1, c)))
        product(joint, shared, into_rows(mine[r][c][1]))
        share(r, c, 1)
        sum_z[r][c][my_z, 0:1, :] = square
        sum_z[r][c][my_z, 1:2, :] = inner(js[c], snd[2 * r + 1][c])

    def stage_image(r, c):
        drain(rcv[2 * r + 1][c], ex_r.at[2 * r + 1, c])
        square = difference(2 * r + 1, c, ds[c])
        product(shared, shared, into_slots(gs[c]))
        sum_z[r][c][my_z, 2:3, :] = square
        sum_z[r][c][my_z, 3:4, :] = inner(ds[c], gs[c])
        if r == 0 and c == 0:
            hear(1)
            assert len(told) <= 2
        for d in z_order:
            z_copy(r, c, d).start()
        product(joint, shared, into_rows(mine[r][c][2]))
        share(r, c, 2)

    def stage_sums(r, c):
        for i in range(2):
            drain(all_of[r][c][i].at[pl.ds(0, harms - 1)], a_r.at[r, c, i])
        drain(sum_z[r][c].at[pl.ds(0, nz - 1)], z_r.at[r, c])
        sum_y[r][c][my_y * harms + harm] = jnp.sum(sum_z[r][c][...], axis=0)
        for peer in plane_peers:
            y_copy(r, c, peer).start()

    def stage_contact(r, c):
        drain(sum_y[r][c].at[pl.ds(0, NY * harms - 1)], y_r.at[r, c])
        value = sum_y[r][c][0:harms]
        for y in range(1, NY):
            value = value + sum_y[r][c][y * harms : (y + 1) * harms]
        square, curve, square_d, curve_d = (value[:, i : i + 1] for i in range(4))
        first = square / (curve + TINY)
        square = square - 4.0 * first * curve + first * first * square_d
        curve = curve - first * square_d + first * first * curve_d
        second = square / (curve + TINY)
        steps[c][0] = jnp.broadcast_to(first + second, (harms, 8, WIDTH))
        steps[c][1] = jnp.broadcast_to(first * second, (harms, 8, WIDTH))
        drain(all_of[r][c][2].at[pl.ds(0, harms - 1)], a_r.at[r, c, 2])
        contact(r, c)
        for d in h_order:
            from_harm(r, c, d).start()
        bc[r][c][rows_of(harm), :] = oc[r][c][harm]

    def stage_step(r, c):
        both, cross = steps[c][0, harm][0:1], steps[c][1, harm][0:1]

        @pl.loop(0, 2 * MAXB)
        def _(k):
            change = cross * ds[c][k] - both * js[c][k]
            ms[c][k] = change if r == 0 else ms[c][k] + change
            if r + 1 < ROUNDS:
                image = snd[2 * r + 1][c][k]
                tn[c][k] = snd[2 * r][c][k] - both * image + cross * gs[c][k]

        if r + 1 < ROUNDS:
            trace, image, second = (mine[r][c][n][...] for n in range(3))
            mine[r + 1][c][0][...] = trace - both * image + cross * second
        else:

            @pl.loop(0, NB)
            def _(b):
                value = jnp.where(tab[3, b] != 0, ms[c][tab[2, b]], 0.0)
                mo[c][b] = value - jnp.where(tab[5, b] != 0, old[c][tab[4, b]], 0.0)

    def stage_force(r, c):
        drain(bc[r][c].at[pl.ds(0, (harms - 1) * part)], a_r.at[r, c, 3])
        for q in range(CB):
            rows = pl.ds(q * BLK, BLK)
            value = bc[r][c][rows, :] * stc[rows, :]
            old[c][q] = value
            if r + 1 < ROUNDS:
                put(q, value)
            else:
                force[q, :, lanes[c]] = value
        if r + 1 < ROUNDS:
            product(shared, joint, into_slots(snd[2 * r + 2][c], tn[c], (2 * r + 2, c)))
            rows = mine[r + 1][c][0]
            product(joint, joint, into_rows(rows, rows))
            share(r + 1, c, 0)
        else:

            @pl.loop(0, NB)
            def _(b):
                value = jnp.where(tab[5, b] != 0, old[c][tab[4, b]], 0.0)
                mult[b, :, lanes[c]] = mo[c][b] - value

    def settle(r, c):
        if r > 0 or c > 0:
            drain(snd[2 * r][c], ex_s.at[2 * r, c])
        drain(snd[2 * r + 1][c], ex_s.at[2 * r + 1, c])
        drain(sum_y[r][c].at[pl.ds(0, NY * harms - 1)], y_s.at[r, c])
        drain(sum_z[r][c].at[pl.ds(0, nz - 1)], z_s.at[r, c])
        for i in range(3):
            drain(mine[r][c][i].at[pl.ds(0, (harms - 1) * part)], a_s.at[r, c, i])

    def settle_last(r, c):
        drain(oc[r][c].at[pl.ds(0, harms - 1)], a_s.at[r, c, 3])

    for r in range(ROUNDS):
        for c in every:
            stage_jump(r, c)
            if r > 0 and c == NCH - 1:
                for old_c in every:
                    settle(r - 1, old_c)
                    settle_last(r - 1, old_c)
        for c in every:
            stage_image(r, c)
        for c in every:
            stage_sums(r, c)
        for c in every:
            stage_contact(r, c)
            stage_step(r, c)
        if r == ROUNDS - 1:
            for c in every:
                settle(r, c)
        for c in every:
            stage_force(r, c)
    for c in every:
        settle_last(ROUNDS - 1, c)


def write_out(mult_v, force_v, mult, force, sem):
    copies = [
        pltpu.make_async_copy(mult_v, mult, sem.at[0]),
        pltpu.make_async_copy(force_v, force, sem.at[1]),
    ]
    for copy in copies:
        copy.start()
    for copy in copies:
        copy.wait()


def per_device(flex, loads, side, partner, contact_blocks, contact_stiff):
    harms = lax.axis_size("harm")
    nz = lax.axis_size("sub") // NY
    part = CROWS // harms
    slots, joint, whole = (
        [pltpu.VMEM((n, BLK, WIDTH), f32)] * NCH for n in (2 * MAXB, CB, NB)
    )
    vmem = lambda *shape: [pltpu.VMEM(shape, f32)] * (NCH * ROUNDS)
    sem = pltpu.SemaphoreType.DMA
    scratch = [
        pltpu.SMEM((1, NB), jnp.int32),
        pltpu.SMEM((1, NB), jnp.int32),
        pltpu.SMEM((1, CB), jnp.int32),
        pltpu.SMEM((6, NB), jnp.int32),
        pltpu.VMEM((1, CROWS), f32),
        pltpu.VMEM((PAIRS, NB, BLK, 128), f32),
        pltpu.VMEM((NB, BLK, COLS), f32),
        pltpu.VMEM((ROWS, ROWS), bf16),
        pltpu.VMEM((ROWS, ROWS), bf16),
        pltpu.VMEM((S_ROWS, 2 * WIDTH), bf16),
        pltpu.VMEM((CROWS, WIDTH), f32),
        pltpu.VMEM((TIMES // 4 + 1, harms, 8, 128), f32),
    ]
    scratch += slots * 5 + [pltpu.VMEM((2, harms, 8, WIDTH), f32)] * NCH + joint + whole
    scratch += slots * (2 * ROUNDS) * 2
    scratch += vmem(nz, 4, WIDTH) + vmem(NY * harms, 4, WIDTH)
    scratch += vmem(harms, part, WIDTH) + vmem(CROWS, WIDTH)
    scratch += vmem(CROWS, WIDTH) * 3 + vmem(harms, part, WIDTH) * 3
    scratch += [sem((6,))]
    scratch += [sem((2 * ROUNDS, NCH))] * 2
    scratch += [sem((ROUNDS, NCH))] * 4
    scratch += [sem((ROUNDS, NCH, 4))] * 2
    scratch += [pltpu.SemaphoreType.REGULAR] * len(relay_steps(nz))
    hbm = pl.BlockSpec(memory_space=pltpu.HBM)
    mult, force = pl.pallas_call(
        functools.partial(kernel, nz, harms),
        out_shape=(
            jax.ShapeDtypeStruct((NB, BLK, COLS), f32),
            jax.ShapeDtypeStruct((CB, BLK, COLS), f32),
        ),
        in_specs=[hbm] * 6,
        out_specs=(OUT, OUT),
        scratch_shapes=scratch,
        compiler_params=pltpu.CompilerParams(
            collective_id=0, has_side_effects=True, vmem_limit_bytes=48 << 20
        ),
    )(
        *(
            pltpu.with_memory_space_constraint(x, pltpu.HBM)
            for x in (
                side,
                partner,
                contact_blocks,
                contact_stiff,
                flex.reshape(NB, BLK, ROWS),
                loads.reshape(NB, BLK, COLS),
            )
        )
    )
    mult, force = pl.pallas_call(
        write_out,
        out_shape=(
            jax.ShapeDtypeStruct((NB, BLK, COLS), f32),
            jax.ShapeDtypeStruct((CB, BLK, COLS), f32),
        ),
        in_specs=[pl.BlockSpec(memory_space=pl.ANY)] * 2,
        out_specs=[pl.BlockSpec(memory_space=pl.ANY)] * 2,
        scratch_shapes=[pltpu.SemaphoreType.DMA((2,))],
        compiler_params=pltpu.CompilerParams(vmem_limit_bytes=1 << 20),
    )(mult, force)
    return mult.reshape(loads.shape), force.reshape(1, 1, CROWS, COLS)


def solution(mesh):
    return jax.shard_map(
        per_device,
        mesh=mesh,
        in_specs=(
            P("sub", "harm", None, None),
            P("sub", "harm", None, None),
            P("sub", None),
            P("sub", None),
            P("sub", None),
            P("sub", None),
        ),
        out_specs=(P("sub", "harm", None, None), P("sub", "harm", None, None)),
        check_vma=False,
    )
```
